32 devices in a mesh: aux: 8 (over y, x, core), half: 4 (over z).
Axes of the slice: x: 2, y: 2, z: 4, core: 2. Of those that a mesh axis runs over, the one named last changes fastest.
Arguments:
- half_slabs: bfloat16 [1536, 4, 8, 960], P('aux', 'half'), may hold values from -1 to 1
- vir_coeff: bfloat16 [960, 384], replicated, may hold values from -0.1875 to 0.1875
- occ_energy: int32 [32], replicated, may hold values from -3000 to -401
- vir_energy: int32 [384], replicated, may hold values from 200 to 3999
- plan: int32 [1, 4], replicated, may hold values from 0 to 31, as said below
Outputs:
- density: bfloat16 [4, 8, 384, 1536], P('half', 'aux')
- pair_energy: float32 [4, 8], P('half', 'aux')
The draws below stay inside these ranges and needn't reach their ends.
Inputs may be any that keep to these rules, and one draw needn't show every extreme that they name: `plan`: all 4 partner indices are distinct.
All inputs are finite; a program needn't handle non-finite values.
Results may differ from the reference program's by a relative error of at most 0.006.
Values may be sent and summed in bfloat16 or wider, within the bound.
No kernel may reach another device: no remote copies, remote signals or barrier semaphores. Data moves between devices by JAX's collectives and lax.ppermute only.
A program may use at most 64 MiB of HBM per device.

```python
import jax
import jax.numpy as jnp
from jax import lax

NAO = 960
NV = 384
NAUX = 1536
OWNERS = 4
ROUNDS = 1
HALVES = 4
OHALF = 8
NOCC = 32


def draw_plan(key, part):
    order = jax.random.permutation(jax.random.fold_in(key, 7), NOCC)
    return order[:ROUNDS * OWNERS].reshape(ROUNDS, OWNERS).astype(jnp.int32)


def touch_ends(values, stream_key, low, top_value):
    longest = values.shape.index(max(values.shape))
    spots = []
    for shift in (0, 1):
        where = [jax.random.randint(jax.random.fold_in(stream_key, axis), (), 0, length) for axis, length in enumerate(values.shape)]
        where[longest] = (where[longest] + shift) % values.shape[longest]
        spots.append(tuple(where))
    return values.at[spots[0]].set(low).at[spots[1]].set(top_value)


def block_levels(stream_key, dims, cuts, low, top_value):
    def one(axis_at, shards_of):
        steps = jax.random.uniform(jax.random.fold_in(jax.random.fold_in(stream_key, 6), axis_at), (shards_of,), jnp.float32, low / len(cuts), top_value / len(cuts))
        return jnp.repeat(jnp.exp(steps), dims[axis_at] // shards_of).reshape((-1,) + (1,) * (len(dims) - axis_at - 1))

    gain = one(*cuts[0])
    for cut in cuts[1:]:
        gain = gain * one(*cut)
    return gain


def bell_draw(stream_key, shape, width, most, pieces=(), kind=jnp.bfloat16):
    result = jax.random.normal(stream_key, shape, jnp.float32) * width
    if len(pieces) > 0:
        result = block_levels(stream_key, shape, pieces, -0.22, 0.18) * result
    return jnp.clip(result, min=-most, max=most).astype(kind)


def setup_inputs(seed: int = 0) -> dict:
    streams_of = jax.random.split(jax.random.key(seed), 6)
    return {
        "half_slabs": bell_draw(streams_of[0], (NAUX, HALVES, OHALF, NAO), 0.16, 1.0, ((0, 8), (1, 4))),
        "vir_coeff": bell_draw(streams_of[1], (NAO, NV), NAO ** -0.5, 0.1875),
        "occ_energy": touch_ends(jax.random.randint(streams_of[2], (NOCC,), -3000, -400), jax.random.fold_in(streams_of[2], 1), -3000, (-400) - 1).astype(jnp.int32),
        "vir_energy": touch_ends(jax.random.randint(streams_of[3], (NV,), 200, 4000), jax.random.fold_in(streams_of[3], 1), 200, 3999).astype(jnp.int32),
        "plan": draw_plan(jax.random.fold_in(streams_of[5], 71), 0),
    }


def transform_half(slab, vir_coeff):
    flat = slab.reshape(NAUX * OHALF, NAO)
    prod = jnp.dot(flat, vir_coeff, preferred_element_type=jnp.float32)
    return jnp.transpose(prod.reshape(NAUX, OHALF, NV), (1, 0, 2)).astype(jnp.bfloat16)


def reference(half_slabs, vir_coeff, occ_energy, vir_energy, plan):
    slabs = jnp.transpose(half_slabs, (1, 0, 2, 3))
    bvir = lax.map(lambda slab: transform_half(slab, vir_coeff), slabs)
    bvir = bvir.reshape(NOCC, NAUX, NV)
    occ_e = occ_energy.astype(jnp.float32) * 0.001
    vir_e = vir_energy.astype(jnp.float32) * 0.001
    flat_sched = plan.reshape(-1).astype(jnp.int32)
    partners = bvir[flat_sched]
    part_e = occ_e[flat_sched]
    count = ROUNDS * OWNERS

    def one(items):
        own, own_e = items
        gamma = jnp.zeros((NV, NAUX), jnp.float32)
        energy = jnp.zeros((), jnp.float32)
        for slot in range(count):
            other = partners[slot]
            kmat = jnp.dot(own.T, other, preferred_element_type=jnp.float32)
            denom = own_e + part_e[slot] - vir_e[:, None] - vir_e[None, :]
            tilde = (2.0 * kmat - kmat.T) / denom
            energy = energy + jnp.sum(kmat * tilde)
            gamma = gamma + jnp.dot(tilde.astype(jnp.bfloat16), other.T, preferred_element_type=jnp.float32)
        return gamma.astype(jnp.bfloat16), energy / (NV * NV)

    gamma, energy = lax.map(one, (bvir, occ_e))
    return gamma.reshape(HALVES, OHALF, NV, NAUX), energy.reshape(HALVES, OHALF)
```

```python
import functools

import jax
import jax.numpy as jnp
from jax import lax
from jax.experimental import pallas as pl
from jax.experimental.pallas import tpu as pltpu
from jax.sharding import PartitionSpec as P

F32 = jnp.float32
BF16 = jnp.bfloat16


def broadcast(x, axis, root):
    mine = lax.axis_index(axis) == root
    return lax.psum(jnp.where(mine, x, jnp.zeros_like(x)), axis)


def any_mesh(half_slabs, vir_coeff, occ_energy, vir_energy, plan):
    local_aux = half_slabs.shape[0]
    ohalf = half_slabs.shape[2]
    flat = half_slabs.reshape(local_aux * ohalf, half_slabs.shape[3])
    prod = jnp.dot(flat, vir_coeff, preferred_element_type=F32)
    transformed = prod.reshape(local_aux, ohalf, vir_coeff.shape[1]).astype(BF16)
    owned = lax.all_to_all(transformed, "aux", split_axis=1, concat_axis=0, tiled=True)
    n_half = lax.axis_size("half")
    aux_index = lax.axis_index("aux")
    half_index = lax.axis_index("half")
    o_dev = owned.shape[1]
    n_virt = owned.shape[2]
    own_start = half_index * ohalf + aux_index * o_dev
    occ_e = occ_energy.astype(F32) * 0.001
    own_e = lax.dynamic_slice_in_dim(occ_e, own_start, o_dev)
    vir_e = vir_energy.astype(F32) * 0.001
    gamma = jnp.zeros((o_dev, n_virt, owned.shape[0]), F32)
    energy = jnp.zeros((o_dev,), F32)
    for partner in plan.reshape(-1):
        part_half = partner // ohalf
        part_aux = partner % ohalf // o_dev
        piece = lax.dynamic_index_in_dim(owned, partner % o_dev, 1, keepdims=False)
        other = broadcast(piece, ("aux", "half"), part_aux * n_half + part_half)
        part_e = lax.dynamic_index_in_dim(occ_e, partner, 0, keepdims=False)
        kmat = jnp.einsum("pia,pb->iab", owned, other, preferred_element_type=F32)
        denom = own_e[:, None, None] + part_e - vir_e[None, :, None] - vir_e[None, None, :]
        tilde = (2.0 * kmat - jnp.swapaxes(kmat, 1, 2)) / denom
        energy = energy + jnp.sum(kmat * tilde, axis=(1, 2))
        gamma = gamma + jnp.einsum("iab,pb->iap", tilde.astype(BF16), other, preferred_element_type=F32)
    return gamma.astype(BF16)[None], (energy / (n_virt * n_virt))[None]


def transform_kernel(plan_ref, pos_ref, slab_ref, coeff_ref, own_ref, *rest):
    lists, acc_ref = rest[:-1], rest[-1]
    n_orb, rows, _ = own_ref.shape
    tiles, _, lanes = acc_ref.shape
    acc = jnp.dot(slab_ref[...], coeff_ref[...], preferred_element_type=F32)
    for t in range(tiles):
        acc_ref[t] = acc[:, t * lanes:(t + 1) * lanes]
    for t in range(tiles):
        cols = slice(t * lanes, (t + 1) * lanes)
        for i in range(n_orb):
            own_ref[i, :, cols] = acc_ref[t, pl.ds(i, rows, stride=n_orb), :].astype(BF16)
    ahead = lax.rem(pl.program_id(0) - pos_ref[0] + len(lists), len(lists))
    for d, list_ref in enumerate(lists):

        @pl.when(ahead == d)
        def _():
            for k in range(list_ref.shape[0]):
                i = lax.rem(plan_ref[0, k], n_orb)
                for t in range(tiles):
                    cols = slice(t * lanes, (t + 1) * lanes)
                    list_ref[k, :, cols] = acc_ref[t, pl.ds(i, rows, stride=n_orb), :].astype(BF16)


def transform(half_slabs, coeff, plan, pos, n_half):
    local_aux, _, n_orb, n_ao = half_slabs.shape
    n_virt = coeff.shape[1]
    count = plan.shape[1]
    rows = local_aux // n_half
    return pl.pallas_call(
        transform_kernel,
        grid_spec=pltpu.PrefetchScalarGridSpec(
            num_scalar_prefetch=2,
            grid=(n_half,),
            in_specs=[
                pl.BlockSpec((rows * n_orb, n_ao), lambda g, *_: (g, 0)),
                pl.BlockSpec((n_ao, n_virt), lambda g, *_: (0, 0)),
            ],
            out_specs=[pl.BlockSpec((n_orb, rows, n_virt), lambda g, *_: (0, g, 0))]
            + [pl.BlockSpec((count, rows, n_virt), lambda g, *_: (0, 0, 0))] * n_half,
            scratch_shapes=[pltpu.VMEM((n_virt // 128, rows * n_orb, 128), F32)],
        ),
        out_shape=[jax.ShapeDtypeStruct((n_orb, local_aux, n_virt), BF16)]
        + [jax.ShapeDtypeStruct((count, rows, n_virt), BF16)] * n_half,
        name="transform",
    )(plan, pos, half_slabs.reshape(local_aux * n_orb, n_ao), coeff)


def merge_kernel(plan_ref, pos_ref, *refs, n_orb):
    lists, out_ref = refs[:-1], refs[-1]
    n_half = len(lists)
    for s in range(out_ref.shape[0]):
        far = lax.rem(pos_ref[0] - lax.div(plan_ref[0, s], n_orb) + n_half, n_half)
        for d, list_ref in enumerate(lists):

            @pl.when(far == d)
            def _():
                out_ref[s] = list_ref[s]


def merge(plan, pos, lists, n_orb):
    smem = pl.BlockSpec(memory_space=pltpu.SMEM)
    vmem = pl.BlockSpec(memory_space=pltpu.VMEM)
    return pl.pallas_call(
        functools.partial(merge_kernel, n_orb=n_orb),
        in_specs=[smem, smem] + [vmem] * len(lists),
        out_specs=vmem,
        out_shape=jax.ShapeDtypeStruct(lists[0].shape, BF16),
        name="merge",
    )(plan, pos, *lists)


def pack_kernel(*refs):
    parts, outs = refs[:-2], refs[-2:]
    per = outs[0].shape[1]
    for d, part in enumerate(parts):
        for g, out in enumerate(outs):
            out[d] = part[g * per:(g + 1) * per]


def pack(parts):
    vmem = pl.BlockSpec(memory_space=pltpu.VMEM)
    count, rows, n_virt = parts[0].shape
    shape = jax.ShapeDtypeStruct((len(parts), count // 2, rows, n_virt), BF16)
    return pl.pallas_call(
        pack_kernel, in_specs=[vmem] * len(parts), out_specs=[vmem] * 2, out_shape=[shape] * 2, name="pack"
    )(*parts)


def pair_kernel(pos_ref, occ_ref, plan_ref, row_ref, col_ref, own_hbm, *rest, n_orb, pieces):
    arrays = rest[:-8]
    dens_ref, energy_ref, own_v, own_t, part_v, acc, sem, own_sem = rest[-8:]
    n_src, rows, n_virt = own_hbm.shape
    z, aux = pos_ref[0], pos_ref[1]
    copies = []
    for a in range(n_src):
        copies.append(pltpu.make_async_copy(own_hbm.at[a], own_v.at[pl.ds(a * rows, rows)], own_sem.at[a]))
    for c in copies:
        c.start()
    waits = []
    i = 0
    for g, group in enumerate(pieces):
        waits.append([])
        for array, entry, bits in group:
            src = arrays[array].at[entry]
            n_half, per, sub, _ = src.shape
            base = lax.bitwise_xor(aux, bits) * rows
            for d in range(n_half):
                at = base + lax.rem(z - d + n_half, n_half) * sub
                c = pltpu.make_async_copy(
                    src.at[d], part_v.at[pl.ds(g * per, per), pl.ds(pl.multiple_of(at, sub), sub)], sem.at[i]
                )
                c.start()
                waits[-1].append(c)
                i += 1
    for c in copies:
        c.wait()
    own_t[...] = jnp.transpose(own_v[...])
    own_e = occ_ref[z * n_orb + aux].astype(F32) * 0.001
    row = row_ref[...].astype(F32) * 0.001
    col = col_ref[...].astype(F32) * 0.001
    energy = jnp.zeros((1, 1), F32)
    for g in range(len(pieces)):
        for c in waits[g]:
            c.wait()
        part = jnp.concatenate([part_v[g * per + s] for s in range(per)], axis=1)
        kk = jnp.dot(own_t[...], part, preferred_element_type=F32)
        tildes = []
        for s in range(per):
            k = kk[:, s * n_virt:(s + 1) * n_virt]
            part_e = occ_ref[plan_ref[0, g * per + s]].astype(F32) * 0.001
            denom = own_e + part_e - col - row
            tilde = (2.0 * k - jnp.transpose(k)) / denom
            energy = energy + jnp.sum(jnp.sum(k * tilde, axis=1, keepdims=True), axis=0, keepdims=True)
            tildes.append(tilde.astype(BF16))
        tb = jnp.concatenate(tildes, axis=1)
        d = lax.dot_general(tb, part, (((1,), (1,)), ((), ())), preferred_element_type=F32)
        if g == 0:
            acc[...] = d
        else:
            dens_ref[...] = (acc[...] + d).astype(BF16)
    energy_ref[...] = energy / (n_virt * n_virt)


def pair_terms(own, arrays, pieces, pos, occ, plan, vir, n_orb):
    n_src, rows, n_virt = own.shape
    n_aux = n_src * rows
    smem = pl.BlockSpec(memory_space=pltpu.SMEM)
    vmem = pl.BlockSpec(memory_space=pltpu.VMEM)
    anym = pl.BlockSpec(memory_space=pl.ANY)
    n_half = arrays[0].shape[1]
    return pl.pallas_call(
        functools.partial(pair_kernel, n_orb=n_orb, pieces=pieces),
        in_specs=[smem] * 3 + [vmem] * 2 + [anym] * (1 + len(arrays)),
        out_specs=[vmem, vmem],
        out_shape=[jax.ShapeDtypeStruct((n_virt, n_aux), BF16), jax.ShapeDtypeStruct((1, 1), F32)],
        scratch_shapes=[
            pltpu.VMEM((n_aux, n_virt), BF16),
            pltpu.VMEM((n_virt, n_aux), BF16),
            pltpu.VMEM((plan.size, n_aux, n_virt), BF16),
            pltpu.VMEM((n_virt, n_aux), F32),
            pltpu.SemaphoreType.DMA((sum(map(len, pieces)) * n_half,)),
            pltpu.SemaphoreType.DMA((n_src,)),
        ],
        compiler_params=pltpu.CompilerParams(vmem_limit_bytes=56 << 20),
        name="pair_terms",
    )(pos, occ, plan, vir.reshape(1, n_virt), vir.reshape(n_virt, 1), own, *arrays)


CORE, X, Y = 1, 2, 4


def swap(x, bit, n):
    return lax.ppermute(x, "aux", [(a, a ^ bit) for a in range(n)])


def shift(x, d, n):
    return lax.ppermute(x, "half", [(h, (h + d) % n) for h in range(n)])


def on_device(half_slabs, vir_coeff, occ_energy, vir_energy, plan):
    n_aux = lax.axis_size("aux")
    n_half = lax.axis_size("half")
    ohalf = half_slabs.shape[2]
    pos = jnp.stack([lax.axis_index("half"), lax.axis_index("aux")]).astype(jnp.int32)
    own8, *lists = transform(half_slabs, vir_coeff, plan, pos, n_half)
    got = [lists[0]] + [shift(lists[d], d, n_half) for d in range(1, n_half)]
    own = lax.all_to_all(own8, "aux", split_axis=0, concat_axis=0, tiled=True)
    mine = merge(plan, pos, got, ohalf)
    pa, pb = pack([mine] + [shift(mine, d, n_half) for d in range(1, n_half)])
    ax = swap(pa, X, n_aux)
    by = swap(pb, Y, n_aux)
    a2 = jnp.stack([pa, ax])
    b2 = jnp.stack([pb, by])
    ay = swap(a2, Y, n_aux)
    bx = swap(b2, X, n_aux)
    arrays = [a2, ay, b2, bx] + [swap(v, CORE, n_aux) for v in (a2, b2, ay, bx)]
    group_a = [(0, 0, 0), (0, 1, X), (1, 0, Y), (1, 1, X ^ Y), (4, 0, 1), (4, 1, X ^ 1), (6, 0, Y ^ 1), (6, 1, X ^ Y ^ 1)]
    group_b = [(2, 0, 0), (2, 1, Y), (3, 0, X), (3, 1, X ^ Y), (5, 0, 1), (5, 1, Y ^ 1), (7, 0, X ^ 1), (7, 1, X ^ Y ^ 1)]
    density, energy = pair_terms(own, arrays, (group_a, group_b), pos, occ_energy, plan, vir_energy, ohalf)
    return density[None, None], energy


def solution(mesh):
    body = on_device if dict(mesh.shape) == {"aux": 8, "half": 4} else any_mesh
    in_specs = (P("aux", "half", None, None), P(), P(), P(), P())
    out_specs = (P("half", "aux", None, None), P("half", "aux"))
    return jax.shard_map(body, mesh=mesh, in_specs=in_specs, out_specs=out_specs, check_vma=False)
```

```python
import functools

import jax
import jax.numpy as jnp
from jax import lax
from jax.experimental import pallas as pl
from jax.experimental.pallas import tpu as pltpu
from jax.sharding import PartitionSpec as P


F32 = jnp.float32
BF16 = jnp.bfloat16


def broadcast(x, axis, root):
    mine = lax.axis_index(axis) == root
    return lax.psum(jnp.where(mine, x, jnp.zeros_like(x)), axis)


def any_mesh(half_slabs, vir_coeff, occ_energy, vir_energy, plan):
    local_aux = half_slabs.shape[0]
    ohalf = half_slabs.shape[2]
    flat = half_slabs.reshape(local_aux * ohalf, half_slabs.shape[3])
    prod = jnp.dot(flat, vir_coeff, preferred_element_type=F32)
    transformed = prod.reshape(local_aux, ohalf, vir_coeff.shape[1]).astype(BF16)
    owned = lax.all_to_all(transformed, "aux", split_axis=1, concat_axis=0, tiled=True)
    n_half = lax.axis_size("half")
    aux_index = lax.axis_index("aux")
    half_index = lax.axis_index("half")
    o_dev = owned.shape[1]
    n_virt = owned.shape[2]
    own_start = half_index * ohalf + aux_index * o_dev
    occ_e = occ_energy.astype(F32) * 0.001
    own_e = lax.dynamic_slice_in_dim(occ_e, own_start, o_dev)
    vir_e = vir_energy.astype(F32) * 0.001
    gamma = jnp.zeros((o_dev, n_virt, owned.shape[0]), F32)
    energy = jnp.zeros((o_dev,), F32)
    for partner in plan.reshape(-1):
        part_half = partner // ohalf
        part_aux = partner % ohalf // o_dev
        piece = lax.dynamic_index_in_dim(owned, partner % o_dev, 1, keepdims=False)
        other = broadcast(piece, ("aux", "half"), part_aux * n_half + part_half)
        part_e = lax.dynamic_index_in_dim(occ_e, partner, 0, keepdims=False)
        kmat = jnp.einsum("pia,pb->iab", owned, other, preferred_element_type=F32)
        denom = own_e[:, None, None] + part_e - vir_e[None, :, None] - vir_e[None, None, :]
        tilde = (2.0 * kmat - jnp.swapaxes(kmat, 1, 2)) / denom
        energy = energy + jnp.sum(kmat * tilde, axis=(1, 2))
        gamma = gamma + jnp.einsum("iab,pb->iap", tilde.astype(BF16), other, preferred_element_type=F32)
    return gamma.astype(BF16)[None], (energy / (n_virt * n_virt))[None]


def transform_kernel(plan_ref, slab_hbm, coeff_hbm, *rest, n_half, order, joined):
    rest = rest[1:] if joined else rest
    own_hbm, lists = rest[0], rest[1:1 + len(order)]
    slab_v, coeff_v, acc_ref, own_v, in_sem, out_sem = rest[1 + len(order):]
    n_orb, _, _ = own_hbm.shape
    tiles, block, lanes = acc_ref.shape
    rows = block // n_orb
    z = lax.axis_index("half")
    loads, saves = [], []
    coeff_copy = pltpu.make_async_copy(coeff_hbm, coeff_v, in_sem.at[len(order)])
    coeff_copy.start()
    for i, d in enumerate(order):
        at = pl.multiple_of(lax.rem(z + d, n_half) * rows, rows)
        at_flat = pl.multiple_of(at * n_orb, block)
        loads.append(pltpu.make_async_copy(slab_hbm.at[pl.ds(at_flat, block)], slab_v.at[i], in_sem.at[i]))
        saves.append(pltpu.make_async_copy(own_v.at[i], own_hbm.at[:, pl.ds(at, rows)], out_sem.at[i]))
        loads[i].start()
    coeff_copy.wait()
    for i in range(len(order)):
        loads[i].wait()
        acc = jnp.dot(slab_v[i], coeff_v[...], preferred_element_type=F32)
        for t in range(tiles):
            acc_ref[t] = acc[:, t * lanes:(t + 1) * lanes]
        for t in range(tiles):
            cols = slice(t * lanes, (t + 1) * lanes)
            for o in range(n_orb):
                own_v[i, o, :, cols] = acc_ref[t, pl.ds(o, rows, stride=n_orb), :].astype(BF16)
        saves[i].start()
        for k in range(lists[i].shape[0]):
            lists[i][k] = own_v[i, lax.rem(plan_ref[0, k], n_orb)]
    for c in saves:
        c.wait()


def transform(half_slabs, coeff, plan, n_half, order, own=()):
    local_aux, _, n_orb, n_ao = half_slabs.shape
    n_virt = coeff.shape[1]
    count = plan.shape[1]
    rows = local_aux // n_half
    n = len(order)
    hbm = pl.BlockSpec(memory_space=pltpu.HBM)
    vmem = pl.BlockSpec(memory_space=pltpu.VMEM)
    return pl.pallas_call(
        functools.partial(transform_kernel, n_half=n_half, order=order, joined=bool(own)),
        in_specs=[pl.BlockSpec(memory_space=pltpu.SMEM), hbm, hbm] + [hbm] * len(own),
        out_specs=[hbm] + [vmem] * n,
        out_shape=[jax.ShapeDtypeStruct((n_orb, local_aux, n_virt), BF16)]
        + [jax.ShapeDtypeStruct((count, rows, n_virt), BF16)] * n,
        scratch_shapes=[
            pltpu.VMEM((n, rows * n_orb, n_ao), BF16),
            pltpu.VMEM((n_ao, n_virt), BF16),
            pltpu.VMEM((n_virt // 128, rows * n_orb, 128), F32),
            pltpu.VMEM((n, n_orb, rows, n_virt), BF16),
            pltpu.SemaphoreType.DMA((n + 1,)),
            pltpu.SemaphoreType.DMA((n,)),
        ],
        input_output_aliases={3: 0} if own else {},
        compiler_params=pltpu.CompilerParams(vmem_limit_bytes=60 << 20),
        name="transform",
    )(plan, half_slabs.reshape(local_aux * n_orb, n_ao), coeff, *own)


def merge_kernel(plan_ref, *refs, n_orb, n_half):
    lists, outs, sem = refs[:n_half], refs[n_half:-1], refs[-1]
    per = outs[0].shape[0]
    z = lax.axis_index("half")

    def copy(d, s):
        return pltpu.make_async_copy(lists[d].at[s], outs[s // per].at[s % per], sem.at[s])

    for s in range(per * len(outs)):
        far = lax.rem(z - lax.div(plan_ref[0, s], n_orb) + n_half, n_half)
        for d in range(n_half):

            @pl.when(far == d)
            def _():
                copy(d, s).start()

    for s in range(per * len(outs)):
        copy(0, s).wait()


def merge(plan, lists, n_orb, per):
    count, rows, n_virt = lists[0].shape
    shape = jax.ShapeDtypeStruct((per, rows, n_virt), BF16)
    return pl.pallas_call(
        functools.partial(merge_kernel, n_orb=n_orb, n_half=len(lists)),
        in_specs=[pl.BlockSpec(memory_space=pltpu.SMEM)] + [pl.BlockSpec(memory_space=pl.ANY)] * len(lists),
        out_specs=[pl.BlockSpec(memory_space=pltpu.VMEM)] * (count // per),
        out_shape=[shape] * (count // per),
        scratch_shapes=[pltpu.SemaphoreType.DMA((count,))],
        compiler_params=pltpu.CompilerParams(vmem_limit_bytes=4 << 20),
        name="merge",
    )(plan, *lists)


def pack_kernel(*refs):
    parts, out = refs[:-1], refs[-1]
    n_half = len(parts)
    per, sub, _ = parts[0].shape
    z = lax.axis_index("half")
    for d, part in enumerate(parts):
        at = pl.multiple_of(lax.rem(z - d + n_half, n_half) * sub, sub)
        for s in range(per):
            out[s, pl.ds(at, sub)] = part[s]


def pack(parts):
    vmem = pl.BlockSpec(memory_space=pltpu.VMEM)
    per, sub, n_virt = parts[0].shape
    return pl.pallas_call(
        pack_kernel,
        in_specs=[vmem] * len(parts),
        out_specs=vmem,
        out_shape=jax.ShapeDtypeStruct((per, len(parts) * sub, n_virt), BF16),
        compiler_params=pltpu.CompilerParams(vmem_limit_bytes=4 << 20),
        name="pack",
    )(*parts)


def join_kernel(*refs):
    parts, out, sem = refs[:-2], refs[-2], refs[-1]
    copies = [pltpu.make_async_copy(part, out.at[i], sem.at[i]) for i, part in enumerate(parts)]
    for c in copies:
        c.start()
    for c in copies:
        c.wait()


def join(parts):
    return pl.pallas_call(
        join_kernel,
        in_specs=[pl.BlockSpec(memory_space=pl.ANY)] * len(parts),
        out_specs=pl.BlockSpec(memory_space=pltpu.VMEM),
        out_shape=jax.ShapeDtypeStruct((len(parts),) + parts[0].shape, BF16),
        scratch_shapes=[pltpu.SemaphoreType.DMA((len(parts),))],
        compiler_params=pltpu.CompilerParams(vmem_limit_bytes=4 << 20),
        name="join",
    )(*parts)


CORE, X, Y = 1, 2, 4


def prep_kernel(own_hbm, own_t, own_v, sem):
    copy = pltpu.make_async_copy(own_hbm, own_v, sem)
    copy.start()
    copy.wait()
    own_t[...] = jnp.transpose(own_v[...].reshape(own_t.shape[1], own_t.shape[0]))


def prep(own):
    n_src, rows, n_virt = own.shape
    return pl.pallas_call(
        prep_kernel,
        in_specs=[pl.BlockSpec(memory_space=pl.ANY)],
        out_specs=pl.BlockSpec(memory_space=pltpu.VMEM),
        out_shape=jax.ShapeDtypeStruct((n_virt, n_src * rows), BF16),
        scratch_shapes=[pltpu.VMEM(own.shape, BF16), pltpu.SemaphoreType.DMA],
        compiler_params=pltpu.CompilerParams(vmem_limit_bytes=8 << 20),
        name="prep",
    )(own)


def amp_kernel(own_t, early, other, out_ref, part_v, sem):
    _, per, rows, _ = early.shape
    aux = lax.axis_index("aux")
    core = lax.rem(aux, 2)
    half = part_v.shape[1]
    side = lax.rem(aux, Y)
    copies = []
    for src, bits in ((early.at[0], 0), (early.at[1 + core], X), (other.at[0], CORE), (other.at[2 - core], X | CORE)):
        at = pl.multiple_of(lax.bitwise_xor(side, bits) * rows, rows)
        copies.append(pltpu.make_async_copy(src, part_v.at[:, pl.ds(at, rows)], sem.at[len(copies)]))
    for c in copies:
        c.start()
    for c in copies:
        c.wait()
    part = jnp.concatenate([part_v[s] for s in range(per)], axis=1)
    own = own_t[:, pl.ds(pl.multiple_of(lax.div(aux, Y) * half, half), half)]
    out_ref[...] = jnp.dot(own, part, preferred_element_type=F32)


def amplitudes(own, early, other):
    _, per, _, n_virt = early.shape
    n_aux = own.shape[1]
    anym = pl.BlockSpec(memory_space=pl.ANY)
    vmem = pl.BlockSpec(memory_space=pltpu.VMEM)
    return pl.pallas_call(
        amp_kernel,
        in_specs=[vmem, anym, anym],
        out_specs=[vmem, vmem],
        out_shape=[
            jax.ShapeDtypeStruct((n_virt, per * n_virt), F32),
            jax.ShapeDtypeStruct((per, n_aux // 2, n_virt), BF16),
        ],
        scratch_shapes=[pltpu.SemaphoreType.DMA((4,))],
        compiler_params=pltpu.CompilerParams(vmem_limit_bytes=12 << 20),
        cost_estimate=pl.CostEstimate(flops=per * n_virt * n_virt * n_aux, bytes_accessed=3 << 20, transcendentals=0),
        name="amplitudes",
    )(own, early, other)


def pair_kernel(occ_ref, plan_ref, row_ref, col_ref, own_t, *rest, n_orb, groups):
    ins = rest[:4 * groups]
    late, late_other = rest[4 * groups:4 * groups + 2]
    dens_ref, energy_ref, part_v, dens_v, sem, out_sem = rest[4 * groups + 2:]
    _, per, rows, n_virt = late.shape
    half = part_v.shape[1]
    z, aux = lax.axis_index("half"), lax.axis_index("aux")
    core = lax.rem(aux, 2)
    here = pl.multiple_of(lax.div(aux, Y) * half, half)
    there = pl.multiple_of((1 - lax.div(aux, Y)) * half, half)
    side = lax.rem(aux, Y)
    copies = []
    for g in range(groups):
        early, other = ins[4 * g:4 * g + 2]
        for src, bits in (
            (early.at[2 - core], 0),
            (late.at[g], X),
            (other.at[1 + core], CORE),
            (late_other.at[g], X | CORE),
        ):
            at = pl.multiple_of(lax.bitwise_xor(side, bits) * rows, rows)
            dst = part_v.at[pl.ds(g * per, per), pl.ds(at, rows)]
            copies.append(pltpu.make_async_copy(src, dst, sem.at[len(copies)]))
    for c in copies:
        c.start()
    own_e = occ_ref[z * n_orb + aux].astype(F32) * 0.001
    row = row_ref[...].astype(F32) * 0.001
    col = col_ref[...].astype(F32) * 0.001
    energy = jnp.zeros((1, 1), F32)
    for c in copies:
        c.wait()
    tildes = []
    for g in range(groups):
        part = jnp.concatenate([part_v[g * per + s] for s in range(per)], axis=1)
        kk = ins[4 * g + 2][...] + jnp.dot(own_t[:, pl.ds(there, half)], part, preferred_element_type=F32)
        for s in range(per):
            k = kk[:, s * n_virt:(s + 1) * n_virt]
            part_e = occ_ref[plan_ref[0, g * per + s]].astype(F32) * 0.001
            denom = own_e + part_e - col - row
            tilde = (2.0 * k - jnp.transpose(k)) / denom
            energy = energy + jnp.sum(jnp.sum(k * tilde, axis=1, keepdims=True), axis=0, keepdims=True)
            tildes.append(tilde.astype(BF16))
    tb = jnp.concatenate(tildes, axis=1)
    saves = []
    for i, (at, parts) in enumerate((
        (here, [ins[4 * g + 3][s] for g in range(groups) for s in range(per)]),
        (there, [part_v[s] for s in range(groups * per)]),
    )):
        part = jnp.concatenate(parts, axis=1)
        total = lax.dot_general(tb, part, (((1,), (1,)), ((), ())), preferred_element_type=F32)
        dens_v[i] = total.astype(BF16)
        saves.append(pltpu.make_async_copy(dens_v.at[i], dens_ref.at[:, pl.ds(at, half)], out_sem.at[i]))
        saves[-1].start()
    for c in saves:
        c.wait()
    energy_ref[...] = energy / (n_virt * n_virt)


def pair_terms(own, ins, late, late_other, occ, plan, vir, n_orb):
    groups, per, _, n_virt = late.shape
    n_aux = own.shape[1]
    smem = pl.BlockSpec(memory_space=pltpu.SMEM)
    vmem = pl.BlockSpec(memory_space=pltpu.VMEM)
    anym = pl.BlockSpec(memory_space=pl.ANY)
    return pl.pallas_call(
        functools.partial(pair_kernel, n_orb=n_orb, groups=groups),
        in_specs=[smem] * 2 + [vmem] * 3 + [anym, anym, vmem, vmem] * groups + [anym] * 2,
        out_specs=[pl.BlockSpec(memory_space=pltpu.HBM), vmem],
        out_shape=[jax.ShapeDtypeStruct((n_virt, n_aux), BF16), jax.ShapeDtypeStruct((1, 1), F32)],
        scratch_shapes=[
            pltpu.VMEM((groups * per, n_aux // 2, n_virt), BF16),
            pltpu.VMEM((2, n_virt, n_aux // 2), BF16),
            pltpu.SemaphoreType.DMA((groups * 4,)),
            pltpu.SemaphoreType.DMA((2,)),
        ],
        compiler_params=pltpu.CompilerParams(vmem_limit_bytes=24 << 20),
        name="pair_terms",
    )(occ, plan, vir.reshape(1, n_virt), vir.reshape(n_virt, 1), own, *ins, late, late_other)


def swap(x, n):
    return lax.ppermute(x, "aux", [(a, a ^ CORE) for a in range(n)])


def plane(x, n, flip):
    return lax.ppermute(x, "aux", [(a, a ^ (Y if (a & CORE) ^ flip else X)) for a in range(n)])


def shift(x, d, n):
    return lax.ppermute(x, "half", [(h, (h + d) % n) for h in range(n)])


GROUPS = 2
FIRST = (1, 2, 3, 0)


def on_device(half_slabs, vir_coeff, occ_energy, vir_energy, plan):
    return stages(half_slabs, vir_coeff, occ_energy, vir_energy, plan)


def stages(half_slabs, vir_coeff, occ_energy, vir_energy, plan):
    n_aux = lax.axis_size("aux")
    n_half = lax.axis_size("half")
    _, _, ohalf, _ = half_slabs.shape
    count = plan.size
    per = count // GROUPS
    own8, *lists_0 = transform(half_slabs, vir_coeff, plan, n_half, FIRST)
    lists = dict(zip(FIRST, lists_0))
    got = [lists[0]]
    for d in range(1, n_half):
        got.append(shift(lists[d], d, n_half))
    own = lax.all_to_all(own8, "aux", split_axis=0, concat_axis=0, tiled=True)
    own = prep(own)
    mine = merge(plan, got, ohalf, per)
    ins, late = [], []
    for g in range(GROUPS):
        parts = [mine[g]]
        for d in range(1, n_half):
            parts.append(shift(mine[g], d, n_half))
        z0 = pack(parts)
        r1 = plane(z0, n_aux, 0)
        r2 = plane(z0, n_aux, 1)
        late.append(plane(r1, n_aux, 1))
        early = join([z0, r1, r2])
        other = swap(early, n_aux)
        ins += [early, other, *amplitudes(own, early, other)]
    late = join(late)
    late_other = swap(late, n_aux)
    density, energy = pair_terms(own, ins, late, late_other, occ_energy, plan, vir_energy, ohalf)
    return density[None, None], energy


def solution(mesh):
    fast = dict(mesh.shape) == {"aux": 8, "half": 4}
    in_specs = (P("aux", "half", None, None), P(), P(), P(), P())
    out_specs = (P("half", "aux", None, None), P("half", "aux"))
    return jax.shard_map(
        on_device if fast else any_mesh, mesh=mesh, in_specs=in_specs, out_specs=out_specs, check_vma=False
    )
```

```python
import functools

import jax
import jax.numpy as jnp
from jax import lax
from jax.experimental import pallas as pl
from jax.experimental.pallas import tpu as pltpu
from jax.sharding import PartitionSpec as P


F32 = jnp.float32
BF16 = jnp.bfloat16


def broadcast(x, axis, root):
    mine = lax.axis_index(axis) == root
    return lax.psum(jnp.where(mine, x, jnp.zeros_like(x)), axis)


def any_mesh(half_slabs, vir_coeff, occ_energy, vir_energy, plan):
    local_aux = half_slabs.shape[0]
    ohalf = half_slabs.shape[2]
    flat = half_slabs.reshape(local_aux * ohalf, half_slabs.shape[3])
    prod = jnp.dot(flat, vir_coeff, preferred_element_type=F32)
    transformed = prod.reshape(local_aux, ohalf, vir_coeff.shape[1]).astype(BF16)
    owned = lax.all_to_all(transformed, "aux", split_axis=1, concat_axis=0, tiled=True)
    n_half = lax.axis_size("half")
    aux_index = lax.axis_index("aux")
    half_index = lax.axis_index("half")
    o_dev = owned.shape[1]
    n_virt = owned.shape[2]
    own_start = half_index * ohalf + aux_index * o_dev
    occ_e = occ_energy.astype(F32) * 0.001
    own_e = lax.dynamic_slice_in_dim(occ_e, own_start, o_dev)
    vir_e = vir_energy.astype(F32) * 0.001
    gamma = jnp.zeros((o_dev, n_virt, owned.shape[0]), F32)
    energy = jnp.zeros((o_dev,), F32)
    for partner in plan.reshape(-1):
        part_half = partner // ohalf
        part_aux = partner % ohalf // o_dev
        piece = lax.dynamic_index_in_dim(owned, partner % o_dev, 1, keepdims=False)
        other = broadcast(piece, ("aux", "half"), part_aux * n_half + part_half)
        part_e = lax.dynamic_index_in_dim(occ_e, partner, 0, keepdims=False)
        kmat = jnp.einsum("pia,pb->iab", owned, other, preferred_element_type=F32)
        denom = own_e[:, None, None] + part_e - vir_e[None, :, None] - vir_e[None, None, :]
        tilde = (2.0 * kmat - jnp.swapaxes(kmat, 1, 2)) / denom
        energy = energy + jnp.sum(kmat * tilde, axis=(1, 2))
        gamma = gamma + jnp.einsum("iab,pb->iap", tilde.astype(BF16), other, preferred_element_type=F32)
    return gamma.astype(BF16)[None], (energy / (n_virt * n_virt))[None]


def partner_half(plan_ref, s, n_orb):
    return lax.div(plan_ref[0, s], n_orb)


def rank_in_half(plan_ref, s, n_orb):
    home = partner_half(plan_ref, s, n_orb)
    return sum([(partner_half(plan_ref, t, n_orb) == home).astype(jnp.int32) for t in range(s)], jnp.int32(0))


def transform_kernel(plan_ref, slab_hbm, coeff_hbm, *rest, n_half, order, chips):
    n = len(order)
    crowd_ref, rest = rest[0], rest[1:]
    outs, lists, spill = rest[:chips], rest[chips:chips + n], rest[chips + n:chips + 2 * n]
    slab_v, coeff_v, acc_ref, own_v, in_sem = rest[chips + 2 * n:]
    cap = lists[0].shape[0]
    count = cap + spill[0].shape[0]
    n_orb = 2 * chips
    aux = lax.axis_index("aux")
    tiles, block, lanes = acc_ref.shape
    rows = block // n_orb
    z = lax.axis_index("half")
    loads, starts = [], []
    coeff_copy = pltpu.make_async_copy(coeff_hbm, coeff_v, in_sem.at[len(order)])
    coeff_copy.start()
    for i, d in enumerate(order):
        at = pl.multiple_of(lax.rem(z + d, n_half) * rows, rows)
        at_flat = pl.multiple_of(at * n_orb, block)
        loads.append(pltpu.make_async_copy(slab_hbm.at[pl.ds(at_flat, block)], slab_v.at[i], in_sem.at[i]))
        starts.append(at)
        loads[i].start()
    ranks = [rank_in_half(plan_ref, s, n_orb) for s in range(count)]
    here = [partner_half(plan_ref, s, n_orb) == z for s in range(count)]
    pick = []
    for k in range(count):
        hits = [
            jnp.where(jnp.logical_and(here[s], ranks[s] == k), lax.rem(plan_ref[0, s], n_orb), 0)
            for s in range(count)
        ]
        pick.append(sum(hits, jnp.int32(0)))
    most = ranks[0]
    for r in ranks[1:]:
        most = jnp.maximum(most, r)
    crowd_ref[0] = (most >= cap).astype(jnp.int32)
    coeff_copy.wait()
    for i in range(len(order)):
        loads[i].wait()
        acc = jnp.dot(slab_v[i], coeff_v[...], preferred_element_type=F32)
        for t in range(tiles):
            acc_ref[t] = acc[:, t * lanes:(t + 1) * lanes]
        for t in range(tiles):
            cols = slice(t * lanes, (t + 1) * lanes)
            for o in range(n_orb):
                own_v[o, :, cols] = acc_ref[t, pl.ds(o, rows, stride=n_orb), :].astype(BF16)
        for r, out in enumerate(outs):
            for j in range(2):
                out[j, pl.ds(starts[i], rows)] = own_v[lax.bitwise_xor(aux, 2 * r + j)]
        for k in range(count):
            if k < cap:
                lists[i][k] = own_v[pick[k]]
            else:
                spill[i][k - cap] = own_v[pick[k]]


def transform(half_slabs, coeff, plan, n_half, order, cap):
    chips = half_slabs.shape[2] // 2
    local_aux, _, n_orb, n_ao = half_slabs.shape
    n_virt = coeff.shape[1]
    count = plan.shape[1]
    rows = local_aux // n_half
    n = len(order)
    hbm = pl.BlockSpec(memory_space=pltpu.HBM)
    vmem = pl.BlockSpec(memory_space=pltpu.VMEM)
    smem = pl.BlockSpec(memory_space=pltpu.SMEM)
    return pl.pallas_call(
        functools.partial(transform_kernel, n_half=n_half, order=order, chips=chips),
        in_specs=[smem, hbm, hbm],
        out_specs=[smem] + [vmem] * (chips + 2 * n),
        out_shape=[
            jax.ShapeDtypeStruct((1,), jnp.int32),
        ]
        + [jax.ShapeDtypeStruct((2, local_aux, n_virt), BF16)] * chips
        + [jax.ShapeDtypeStruct((cap, rows, n_virt), BF16)] * n
        + [jax.ShapeDtypeStruct((count - cap, rows, n_virt), BF16)] * n,
        scratch_shapes=[
            pltpu.VMEM((n, rows * n_orb, n_ao), BF16),
            pltpu.VMEM((n_ao, n_virt), BF16),
            pltpu.VMEM((n_virt // 128, rows * n_orb, 128), F32),
            pltpu.VMEM((n_orb, rows, n_virt), BF16),
            pltpu.SemaphoreType.DMA((n + 1,)),
        ],
        compiler_params=pltpu.CompilerParams(vmem_limit_bytes=60 << 20),
        name="transform",
    )(plan, half_slabs.reshape(local_aux * n_orb, n_ao), coeff)


def merge_kernel(plan_ref, *refs, n_orb, n_half, spilled):
    n_in = 2 * n_half if spilled else n_half
    lists, outs, sem = refs[:n_in], refs[n_in:-1], refs[-1]
    cap = lists[0].shape[0]
    per = outs[0].shape[0]
    z = lax.axis_index("half")
    for s in range(per * len(outs)):
        far = lax.rem(z - partner_half(plan_ref, s, n_orb) + n_half, n_half)
        rank = rank_in_half(plan_ref, s, n_orb)
        for d in range(n_half):

            @pl.when(jnp.logical_and(far == d, rank < cap))
            def _():
                src = lists[d].at[jnp.minimum(rank, cap - 1)]
                pltpu.make_async_copy(src, outs[s // per].at[s % per], sem.at[s]).start()

            if spilled:

                @pl.when(jnp.logical_and(far == d, rank >= cap))
                def _():
                    src = lists[n_half + d].at[jnp.maximum(rank - cap, 0)]
                    pltpu.make_async_copy(src, outs[s // per].at[s % per], sem.at[s]).start()

    for s in range(per * len(outs)):
        pltpu.make_async_copy(lists[0].at[0], outs[s // per].at[s % per], sem.at[s]).wait()


def merge(plan, lists, n_orb, n_half, per):
    count = plan.shape[1]
    _, rows, n_virt = lists[0].shape
    shape = jax.ShapeDtypeStruct((per, rows, n_virt), BF16)
    return pl.pallas_call(
        functools.partial(merge_kernel, n_orb=n_orb, n_half=n_half, spilled=len(lists) > n_half),
        in_specs=[pl.BlockSpec(memory_space=pltpu.SMEM)] + [pl.BlockSpec(memory_space=pl.ANY)] * len(lists),
        out_specs=[pl.BlockSpec(memory_space=pltpu.VMEM)] * (count // per),
        out_shape=[shape] * (count // per),
        scratch_shapes=[pltpu.SemaphoreType.DMA((count,))],
        compiler_params=pltpu.CompilerParams(vmem_limit_bytes=4 << 20),
        name="merge",
    )(plan, *lists)


def pack_kernel(*refs):
    parts, out = refs[:-1], refs[-1]
    n_half = len(parts)
    per, sub, _ = parts[0].shape
    z = lax.axis_index("half")
    for d, part in enumerate(parts):
        at = pl.multiple_of(lax.rem(z - d + n_half, n_half) * sub, sub)
        for s in range(per):
            out[s, pl.ds(at, sub)] = part[s]


def pack(parts):
    vmem = pl.BlockSpec(memory_space=pltpu.VMEM)
    per, sub, n_virt = parts[0].shape
    return pl.pallas_call(
        pack_kernel,
        in_specs=[vmem] * len(parts),
        out_specs=vmem,
        out_shape=jax.ShapeDtypeStruct((per, len(parts) * sub, n_virt), BF16),
        compiler_params=pltpu.CompilerParams(vmem_limit_bytes=4 << 20),
        name="pack",
    )(*parts)


def join_kernel(*refs, entry):
    parts, out, sem = refs[:-2], refs[-2], refs[-1]
    parts = parts if entry is None else [part.at[entry] for part in parts]
    copies = [pltpu.make_async_copy(part, out.at[i], sem.at[i]) for i, part in enumerate(parts)]
    for c in copies:
        c.start()
    for c in copies:
        c.wait()


def join(parts, entry=None):
    shape = parts[0].shape if entry is None else parts[0].shape[1:]
    return pl.pallas_call(
        functools.partial(join_kernel, entry=entry),
        in_specs=[pl.BlockSpec(memory_space=pl.ANY)] * len(parts),
        out_specs=pl.BlockSpec(memory_space=pltpu.VMEM),
        out_shape=jax.ShapeDtypeStruct((len(parts),) + shape, BF16),
        scratch_shapes=[pltpu.SemaphoreType.DMA((len(parts),))],
        compiler_params=pltpu.CompilerParams(vmem_limit_bytes=4 << 20),
        name="join",
    )(*parts)


CORE, X, Y = 1, 2, 4


def prep_kernel(*refs):
    near, other, own_t, own_v, sem = refs[:-4], refs[-4], refs[-3], refs[-2], refs[-1]
    aux = lax.axis_index("aux")
    copies = []
    for r in range(len(near)):
        for src, bits in ((near[r].at[0], 2 * r), (other.at[r], 2 * r + 1)):
            at = lax.bitwise_xor(aux, bits)
            copies.append(pltpu.make_async_copy(src, own_v.at[at], sem.at[len(copies)]))
    for c in copies:
        c.start()
    for c in copies:
        c.wait()
    own_t[...] = jnp.transpose(own_v[...].reshape(own_t.shape[1], own_t.shape[0]))


def prep(near, other):
    chips, rows, n_virt = other.shape
    return pl.pallas_call(
        prep_kernel,
        in_specs=[pl.BlockSpec(memory_space=pl.ANY)] * (chips + 1),
        out_specs=pl.BlockSpec(memory_space=pltpu.VMEM),
        out_shape=jax.ShapeDtypeStruct((n_virt, 2 * chips * rows), BF16),
        scratch_shapes=[pltpu.VMEM((2 * chips, rows, n_virt), BF16), pltpu.SemaphoreType.DMA((2 * chips,))],
        compiler_params=pltpu.CompilerParams(vmem_limit_bytes=8 << 20),
        name="prep",
    )(*near, other)


def amp_kernel(own_t, early, other, out_ref, part_v, sem):
    _, per, rows, _ = early.shape
    aux = lax.axis_index("aux")
    core = lax.rem(aux, 2)
    half = part_v.shape[1]
    side = lax.rem(aux, Y)
    copies = []
    for src, bits in ((early.at[0], 0), (early.at[1 + core], X), (other.at[0], CORE), (other.at[2 - core], X | CORE)):
        at = pl.multiple_of(lax.bitwise_xor(side, bits) * rows, rows)
        copies.append(pltpu.make_async_copy(src, part_v.at[:, pl.ds(at, rows)], sem.at[len(copies)]))
    for c in copies:
        c.start()
    for c in copies:
        c.wait()
    part = jnp.concatenate([part_v[s] for s in range(per)], axis=1)
    own = own_t[:, pl.ds(pl.multiple_of(lax.div(aux, Y) * half, half), half)]
    out_ref[...] = jnp.dot(own, part, preferred_element_type=F32)


def amplitudes(own, early, other):
    _, per, _, n_virt = early.shape
    n_aux = own.shape[1]
    anym = pl.BlockSpec(memory_space=pl.ANY)
    vmem = pl.BlockSpec(memory_space=pltpu.VMEM)
    return pl.pallas_call(
        amp_kernel,
        in_specs=[vmem, anym, anym],
        out_specs=[vmem, vmem],
        out_shape=[
            jax.ShapeDtypeStruct((n_virt, per * n_virt), F32),
            jax.ShapeDtypeStruct((per, n_aux // 2, n_virt), BF16),
        ],
        scratch_shapes=[pltpu.SemaphoreType.DMA((4,))],
        compiler_params=pltpu.CompilerParams(vmem_limit_bytes=12 << 20),
        cost_estimate=pl.CostEstimate(flops=per * n_virt * n_virt * n_aux, bytes_accessed=3 << 20, transcendentals=0),
        name="amplitudes",
    )(own, early, other)


def pair_kernel(occ_ref, plan_ref, row_ref, col_ref, own_t, *rest, n_orb, groups):
    ins = rest[:4 * groups]
    late, late_other = rest[4 * groups:4 * groups + 2]
    dens_ref, energy_ref, part_v, dens_v, sem, out_sem = rest[4 * groups + 2:]
    _, per, rows, n_virt = late.shape
    half = part_v.shape[1]
    z, aux = lax.axis_index("half"), lax.axis_index("aux")
    core = lax.rem(aux, 2)
    here = pl.multiple_of(lax.div(aux, Y) * half, half)
    there = pl.multiple_of((1 - lax.div(aux, Y)) * half, half)
    side = lax.rem(aux, Y)
    copies = []
    for g in range(groups):
        early, other = ins[4 * g:4 * g + 2]
        for src, bits in (
            (early.at[2 - core], 0),
            (late.at[g], X),
            (other.at[1 + core], CORE),
            (late_other.at[g], X | CORE),
        ):
            at = pl.multiple_of(lax.bitwise_xor(side, bits) * rows, rows)
            dst = part_v.at[pl.ds(g * per, per), pl.ds(at, rows)]
            copies.append(pltpu.make_async_copy(src, dst, sem.at[len(copies)]))
    for c in copies:
        c.start()
    own_e = occ_ref[z * n_orb + aux].astype(F32) * 0.001
    row = row_ref[...].astype(F32) * 0.001
    col = col_ref[...].astype(F32) * 0.001
    energy = jnp.zeros((1, 1), F32)
    for c in copies:
        c.wait()
    tildes = []
    for g in range(groups):
        part = jnp.concatenate([part_v[g * per + s] for s in range(per)], axis=1)
        kk = ins[4 * g + 2][...] + jnp.dot(own_t[:, pl.ds(there, half)], part, preferred_element_type=F32)
        for s in range(per):
            k = kk[:, s * n_virt:(s + 1) * n_virt]
            part_e = occ_ref[plan_ref[0, g * per + s]].astype(F32) * 0.001
            denom = own_e + part_e - col - row
            tilde = (2.0 * k - jnp.transpose(k)) / denom
            energy = energy + jnp.sum(jnp.sum(k * tilde, axis=1, keepdims=True), axis=0, keepdims=True)
            tildes.append(tilde.astype(BF16))
    tb = jnp.concatenate(tildes, axis=1)
    saves = []
    for i, (at, parts) in enumerate((
        (here, [ins[4 * g + 3][s] for g in range(groups) for s in range(per)]),
        (there, [part_v[s] for s in range(groups * per)]),
    )):
        part = jnp.concatenate(parts, axis=1)
        total = lax.dot_general(tb, part, (((1,), (1,)), ((), ())), preferred_element_type=F32)
        dens_v[i] = total.astype(BF16)
        saves.append(pltpu.make_async_copy(dens_v.at[i], dens_ref.at[:, pl.ds(at, half)], out_sem.at[i]))
        saves[-1].start()
    for c in saves:
        c.wait()
    energy_ref[...] = energy / (n_virt * n_virt)


def pair_terms(own, ins, late, late_other, occ, plan, vir, n_orb):
    groups, per, _, n_virt = late.shape
    n_aux = own.shape[1]
    smem = pl.BlockSpec(memory_space=pltpu.SMEM)
    vmem = pl.BlockSpec(memory_space=pltpu.VMEM)
    anym = pl.BlockSpec(memory_space=pl.ANY)
    return pl.pallas_call(
        functools.partial(pair_kernel, n_orb=n_orb, groups=groups),
        in_specs=[smem] * 2 + [vmem] * 3 + [anym, anym, vmem, vmem] * groups + [anym] * 2,
        out_specs=[pl.BlockSpec(memory_space=pltpu.HBM), vmem],
        out_shape=[jax.ShapeDtypeStruct((n_virt, n_aux), BF16), jax.ShapeDtypeStruct((1, 1), F32)],
        scratch_shapes=[
            pltpu.VMEM((groups * per, n_aux // 2, n_virt), BF16),
            pltpu.VMEM((2, n_virt, n_aux // 2), BF16),
            pltpu.SemaphoreType.DMA((groups * 4,)),
            pltpu.SemaphoreType.DMA((2,)),
        ],
        compiler_params=pltpu.CompilerParams(vmem_limit_bytes=24 << 20),
        name="pair_terms",
    )(occ, plan, vir.reshape(1, n_virt), vir.reshape(n_virt, 1), own, *ins, late, late_other)


def swap(x, n):
    return lax.ppermute(x, "aux", [(a, a ^ CORE) for a in range(n)])


def plane(x, n, flip):
    return lax.ppermute(x, "aux", [(a, a ^ (Y if (a & CORE) ^ flip else X)) for a in range(n)])


def shift(x, d, n):
    return lax.ppermute(x, "half", [(h, (h + d) % n) for h in range(n)])


GROUPS = 2


def on_device(half_slabs, vir_coeff, occ_energy, vir_energy, plan):
    return stages(half_slabs, vir_coeff, occ_energy, vir_energy, plan)


def stages(half_slabs, vir_coeff, occ_energy, vir_energy, plan):
    n_aux = lax.axis_size("aux")
    n_half = lax.axis_size("half")
    _, _, ohalf, _ = half_slabs.shape
    count = plan.size
    per = count // GROUPS
    cap = max(1, count // 2)
    order = tuple(range(1, n_half)) + (0,)
    crowd, *lists = transform(half_slabs, vir_coeff, plan, n_half, order, cap)
    near, lists = lists[:n_aux // 2], lists[n_aux // 2:]
    lists, spill = lists[:n_half], lists[n_half:]
    lists, spill = [lists[-1]] + lists[:-1], [spill[-1]] + spill[:-1]
    got = [lists[0]]
    for d in range(1, n_half):
        got.append(shift(lists[d], d, n_half))
    for r in range(1, n_aux // 2):
        near[r] = lax.ppermute(near[r], "aux", [(a, a ^ (2 * r)) for a in range(n_aux)])
    other = join(near, 1)
    other = swap(other, n_aux)
    own = prep(near, other)

    def roomy(got, spill):
        return merge(plan, got, ohalf, n_half, per)

    def crowded(got, spill):
        more = [spill[0]] + [shift(spill[d], d, n_half) for d in range(1, n_half)]
        return merge(plan, got + more, ohalf, n_half, per)

    mine = lax.switch(crowd[0], [roomy, crowded], got, spill)
    ins, late = [], []
    for g in range(GROUPS):
        parts = [mine[g]]
        for d in range(1, n_half):
            parts.append(shift(mine[g], d, n_half))
        z0 = pack(parts)
        r1 = plane(z0, n_aux, 0)
        r2 = plane(z0, n_aux, 1)
        late.append(plane(r1, n_aux, 1))
        early = join([z0, r1, r2])
        other = swap(early, n_aux)
        ins += [early, other, *amplitudes(own, early, other)]
    late = join(late)
    late_other = swap(late, n_aux)
    density, energy = pair_terms(own, ins, late, late_other, occ_energy, plan, vir_energy, ohalf)
    return density[None, None], energy


def solution(mesh):
    fast = dict(mesh.shape) == {"aux": 8, "half": 4}
    in_specs = (P("aux", "half", None, None), P(), P(), P(), P())
    out_specs = (P("half", "aux", None, None), P("half", "aux"))
    return jax.shard_map(
        on_device if fast else any_mesh, mesh=mesh, in_specs=in_specs, out_specs=out_specs, check_vma=False
    )
```

```python
import functools

import jax
import jax.numpy as jnp
from jax import lax
from jax.experimental import pallas as pl
from jax.experimental.pallas import tpu as pltpu
from jax.sharding import PartitionSpec as P


F32 = jnp.float32
BF16 = jnp.bfloat16


def broadcast(x, axis, root):
    mine = lax.axis_index(axis) == root
    return lax.psum(jnp.where(mine, x, jnp.zeros_like(x)), axis)


def any_mesh(half_slabs, vir_coeff, occ_energy, vir_energy, plan):
    local_aux = half_slabs.shape[0]
    ohalf = half_slabs.shape[2]
    flat = half_slabs.reshape(local_aux * ohalf, half_slabs.shape[3])
    prod = jnp.dot(flat, vir_coeff, preferred_element_type=F32)
    transformed = prod.reshape(local_aux, ohalf, vir_coeff.shape[1]).astype(BF16)
    owned = lax.all_to_all(transformed, "aux", split_axis=1, concat_axis=0, tiled=True)
    n_half = lax.axis_size("half")
    aux_index = lax.axis_index("aux")
    half_index = lax.axis_index("half")
    o_dev = owned.shape[1]
    n_virt = owned.shape[2]
    own_start = half_index * ohalf + aux_index * o_dev
    occ_e = occ_energy.astype(F32) * 0.001
    own_e = lax.dynamic_slice_in_dim(occ_e, own_start, o_dev)
    vir_e = vir_energy.astype(F32) * 0.001
    gamma = jnp.zeros((o_dev, n_virt, owned.shape[0]), F32)
    energy = jnp.zeros((o_dev,), F32)
    for partner in plan.reshape(-1):
        part_half = partner // ohalf
        part_aux = partner % ohalf // o_dev
        piece = lax.dynamic_index_in_dim(owned, partner % o_dev, 1, keepdims=False)
        other = broadcast(piece, ("aux", "half"), part_aux * n_half + part_half)
        part_e = lax.dynamic_index_in_dim(occ_e, partner, 0, keepdims=False)
        kmat = jnp.einsum("pia,pb->iab", owned, other, preferred_element_type=F32)
        denom = own_e[:, None, None] + part_e - vir_e[None, :, None] - vir_e[None, None, :]
        tilde = (2.0 * kmat - jnp.swapaxes(kmat, 1, 2)) / denom
        energy = energy + jnp.sum(kmat * tilde, axis=(1, 2))
        gamma = gamma + jnp.einsum("iab,pb->iap", tilde.astype(BF16), other, preferred_element_type=F32)
    return gamma.astype(BF16)[None], (energy / (n_virt * n_virt))[None]


def partner_half(plan_ref, s, n_orb):
    return lax.div(plan_ref[0, s], n_orb)


def rank_in_half(plan_ref, s, n_orb):
    home = partner_half(plan_ref, s, n_orb)
    return sum([(partner_half(plan_ref, t, n_orb) == home).astype(jnp.int32) for t in range(s)], jnp.int32(0))


def transform_kernel(plan_ref, slab_hbm, coeff_hbm, *rest, n_half, order, chips):
    n = len(order)
    crowd_ref, rest = rest[0], rest[1:]
    outs, lists, spill = rest[:chips], rest[chips:chips + n], rest[chips + n:chips + 2 * n]
    slab_v, coeff_v, acc_ref, own_v, in_sem = rest[chips + 2 * n:]
    cap = lists[0].shape[0]
    count = cap + spill[0].shape[0]
    n_orb = 2 * chips
    aux = lax.axis_index("aux")
    tiles, block, lanes = acc_ref.shape
    rows = block // n_orb
    z = lax.axis_index("half")
    loads, starts = [], []
    coeff_copy = pltpu.make_async_copy(coeff_hbm, coeff_v, in_sem.at[len(order)])
    coeff_copy.start()
    for i, d in enumerate(order):
        at = pl.multiple_of(lax.rem(z + d, n_half) * rows, rows)
        at_flat = pl.multiple_of(at * n_orb, block)
        loads.append(pltpu.make_async_copy(slab_hbm.at[pl.ds(at_flat, block)], slab_v.at[i], in_sem.at[i]))
        starts.append(at)
        loads[i].start()
    ranks = [rank_in_half(plan_ref, s, n_orb) for s in range(count)]
    here = [partner_half(plan_ref, s, n_orb) == z for s in range(count)]
    pick = []
    for k in range(count):
        hits = [
            jnp.where(jnp.logical_and(here[s], ranks[s] == k), lax.rem(plan_ref[0, s], n_orb), 0)
            for s in range(count)
        ]
        pick.append(sum(hits, jnp.int32(0)))
    most = ranks[0]
    for r in ranks[1:]:
        most = jnp.maximum(most, r)
    crowd_ref[0] = (most >= cap).astype(jnp.int32)
    coeff_copy.wait()
    for i in range(len(order)):
        loads[i].wait()
        acc = jnp.dot(slab_v[i], coeff_v[...], preferred_element_type=F32)
        for t in range(tiles):
            acc_ref[t] = acc[:, t * lanes:(t + 1) * lanes]
        for t in range(tiles):
            cols = slice(t * lanes, (t + 1) * lanes)
            for o in range(n_orb):
                own_v[o, :, cols] = acc_ref[t, pl.ds(o, rows, stride=n_orb), :].astype(BF16)
        for r, out in enumerate(outs):
            for j in range(2):
                out[j, pl.ds(starts[i], rows)] = own_v[lax.bitwise_xor(aux, 2 * r + j)]
        for k in range(count):
            if k < cap:
                lists[i][k] = own_v[pick[k]]
            else:
                spill[i][k - cap] = own_v[pick[k]]


def transform(half_slabs, coeff, plan, n_half, order, cap):
    chips = half_slabs.shape[2] // 2
    local_aux, _, n_orb, n_ao = half_slabs.shape
    n_virt = coeff.shape[1]
    count = plan.shape[1]
    rows = local_aux // n_half
    n = len(order)
    hbm = pl.BlockSpec(memory_space=pltpu.HBM)
    vmem = pl.BlockSpec(memory_space=pltpu.VMEM)
    smem = pl.BlockSpec(memory_space=pltpu.SMEM)
    return pl.pallas_call(
        functools.partial(transform_kernel, n_half=n_half, order=order, chips=chips),
        in_specs=[smem, hbm, hbm],
        out_specs=[smem] + [vmem] * (chips + 2 * n),
        out_shape=[
            jax.ShapeDtypeStruct((1,), jnp.int32),
        ]
        + [jax.ShapeDtypeStruct((2, local_aux, n_virt), BF16)] * chips
        + [jax.ShapeDtypeStruct((cap, rows, n_virt), BF16)] * n
        + [jax.ShapeDtypeStruct((count - cap, rows, n_virt), BF16)] * n,
        scratch_shapes=[
            pltpu.VMEM((n, rows * n_orb, n_ao), BF16),
            pltpu.VMEM((n_ao, n_virt), BF16),
            pltpu.VMEM((n_virt // 128, rows * n_orb, 128), F32),
            pltpu.VMEM((n_orb, rows, n_virt), BF16),
            pltpu.SemaphoreType.DMA((n + 1,)),
        ],
        compiler_params=pltpu.CompilerParams(vmem_limit_bytes=20 << 20),
        name="transform",
    )(
        plan,
        pltpu.with_memory_space_constraint(half_slabs.reshape(local_aux * n_orb, n_ao), pltpu.HBM),
        pltpu.with_memory_space_constraint(coeff, pltpu.HBM),
    )


def merge_kernel(plan_ref, *refs, n_orb, n_half, spilled):
    n_in = 2 * n_half if spilled else n_half
    lists, outs, sem = refs[:n_in], refs[n_in:-1], refs[-1]
    cap = lists[0].shape[0]
    per = outs[0].shape[0]
    z = lax.axis_index("half")
    for s in range(per * len(outs)):
        far = lax.rem(z - partner_half(plan_ref, s, n_orb) + n_half, n_half)
        rank = rank_in_half(plan_ref, s, n_orb)
        for d in range(n_half):

            @pl.when(jnp.logical_and(far == d, rank < cap))
            def _():
                src = lists[d].at[jnp.minimum(rank, cap - 1)]
                pltpu.make_async_copy(src, outs[s // per].at[s % per], sem.at[s]).start()

            if spilled:

                @pl.when(jnp.logical_and(far == d, rank >= cap))
                def _():
                    src = lists[n_half + d].at[jnp.maximum(rank - cap, 0)]
                    pltpu.make_async_copy(src, outs[s // per].at[s % per], sem.at[s]).start()

    for s in range(per * len(outs)):
        pltpu.make_async_copy(lists[0].at[0], outs[s // per].at[s % per], sem.at[s]).wait()


def merge(plan, lists, n_orb, n_half, per):
    count = plan.shape[1]
    _, rows, n_virt = lists[0].shape
    shape = jax.ShapeDtypeStruct((per, rows, n_virt), BF16)
    return pl.pallas_call(
        functools.partial(merge_kernel, n_orb=n_orb, n_half=n_half, spilled=len(lists) > n_half),
        in_specs=[pl.BlockSpec(memory_space=pltpu.SMEM)] + [pl.BlockSpec(memory_space=pl.ANY)] * len(lists),
        out_specs=[pl.BlockSpec(memory_space=pltpu.VMEM)] * (count // per),
        out_shape=[shape] * (count // per),
        scratch_shapes=[pltpu.SemaphoreType.DMA((count,))],
        compiler_params=pltpu.CompilerParams(vmem_limit_bytes=4 << 20),
        name="merge",
    )(plan, *lists)


def pack_kernel(*refs):
    parts, out = refs[:-1], refs[-1]
    n_half = len(parts)
    per, sub, _ = parts[0].shape
    z = lax.axis_index("half")
    for d, part in enumerate(parts):
        at = pl.multiple_of(lax.rem(z - d + n_half, n_half) * sub, sub)
        for s in range(per):
            out[s, pl.ds(at, sub)] = part[s]


def pack(parts):
    vmem = pl.BlockSpec(memory_space=pltpu.VMEM)
    per, sub, n_virt = parts[0].shape
    return pl.pallas_call(
        pack_kernel,
        in_specs=[vmem] * len(parts),
        out_specs=vmem,
        out_shape=jax.ShapeDtypeStruct((per, len(parts) * sub, n_virt), BF16),
        compiler_params=pltpu.CompilerParams(vmem_limit_bytes=4 << 20),
        name="pack",
    )(*parts)


def join_kernel(*refs, entry):
    parts, out, sem = refs[:-2], refs[-2], refs[-1]
    parts = parts if entry is None else [part.at[entry] for part in parts]
    copies = [pltpu.make_async_copy(part, out.at[i], sem.at[i]) for i, part in enumerate(parts)]
    for c in copies:
        c.start()
    for c in copies:
        c.wait()


def join(parts, entry=None):
    shape = parts[0].shape if entry is None else parts[0].shape[1:]
    return pl.pallas_call(
        functools.partial(join_kernel, entry=entry),
        in_specs=[pl.BlockSpec(memory_space=pl.ANY)] * len(parts),
        out_specs=pl.BlockSpec(memory_space=pltpu.VMEM),
        out_shape=jax.ShapeDtypeStruct((len(parts),) + shape, BF16),
        scratch_shapes=[pltpu.SemaphoreType.DMA((len(parts),))],
        compiler_params=pltpu.CompilerParams(vmem_limit_bytes=4 << 20),
        name="join",
    )(*parts)


CORE, X, Y = 1, 2, 4


def prep_kernel(*refs):
    near, other, own_t = refs[:-2], refs[-2], refs[-1]
    chips = len(near)
    aux = lax.axis_index("aux")
    core = lax.rem(aux, 2)
    width = 2 * other.shape[1]
    for r in range(chips):
        mine, theirs = near[r][0], other[r]
        pair = jnp.concatenate([jnp.where(core == 0, mine, theirs), jnp.where(core == 0, theirs, mine)], axis=0)
        at = pl.multiple_of(lax.bitwise_xor(lax.div(aux, 2), r) * width, width)
        own_t[:, pl.ds(at, width)] = jnp.transpose(pair)


def prep(near, other):
    _, rows, n_virt = other.shape
    vmem = pl.BlockSpec(memory_space=pltpu.VMEM)
    return pl.pallas_call(
        prep_kernel,
        in_specs=[vmem] * (len(near) + 1),
        out_specs=vmem,
        out_shape=jax.ShapeDtypeStruct((n_virt, 2 * len(near) * rows), BF16),
        compiler_params=pltpu.CompilerParams(vmem_limit_bytes=8 << 20),
        name="prep",
    )(*near, other)


def amp_kernel(own_t, early, other, k_ref, here_ref, beside_ref, sem):
    _, per, rows, _ = early.shape
    aux = lax.axis_index("aux")
    core = lax.rem(aux, 2)
    half, quarter = here_ref.shape[1], beside_ref.shape[1]
    side = lax.rem(aux, Y)
    copies = []
    for src, block, out in (
        (early.at[0], side, here_ref),
        (early.at[1 + core], lax.bitwise_xor(side, X), here_ref),
        (other.at[0], lax.bitwise_xor(side, CORE), here_ref),
        (other.at[2 - core], lax.bitwise_xor(side, X | CORE), here_ref),
        (early.at[2 - core], core, beside_ref),
        (other.at[1 + core], 1 - core, beside_ref),
    ):
        at = pl.multiple_of(block * rows, rows)
        copies.append(pltpu.make_async_copy(src, out.at[:, pl.ds(at, rows)], sem.at[len(copies)]))
    for c in copies:
        c.start()
    for c in copies:
        c.wait()
    here = pl.multiple_of(lax.div(aux, Y) * half, half)
    beside = pl.multiple_of(lax.bitwise_xor(lax.div(aux, 2), Y // 2) * quarter, quarter)
    part = jnp.concatenate([here_ref[s] for s in range(per)], axis=1)
    k = jnp.dot(own_t[:, pl.ds(here, half)], part, preferred_element_type=F32)
    part = jnp.concatenate([beside_ref[s] for s in range(per)], axis=1)
    k_ref[...] = k + jnp.dot(own_t[:, pl.ds(beside, quarter)], part, preferred_element_type=F32)


def amplitudes(own, early, other):
    _, per, _, n_virt = early.shape
    n_aux = own.shape[1]
    anym = pl.BlockSpec(memory_space=pl.ANY)
    vmem = pl.BlockSpec(memory_space=pltpu.VMEM)
    return pl.pallas_call(
        amp_kernel,
        in_specs=[vmem, anym, anym],
        out_specs=[vmem] * 3,
        out_shape=[
            jax.ShapeDtypeStruct((n_virt, per * n_virt), F32),
            jax.ShapeDtypeStruct((per, n_aux // 2, n_virt), BF16),
            jax.ShapeDtypeStruct((per, n_aux // 4, n_virt), BF16),
        ],
        scratch_shapes=[pltpu.SemaphoreType.DMA((6,))],
        compiler_params=pltpu.CompilerParams(vmem_limit_bytes=12 << 20),
        cost_estimate=pl.CostEstimate(flops=per * n_virt * n_virt * n_aux, bytes_accessed=3 << 20, transcendentals=0),
        name="amplitudes",
    )(own, early, other)


def pair_kernel(occ_ref, plan_ref, row_ref, col_ref, own_t, *rest, n_orb, groups):
    ins = rest[:3 * groups]
    late, late_other, dens_ref, energy_ref, part_v, dens_v, sem, out_sem = rest[3 * groups:]
    _, per, rows, n_virt = late.shape
    quarter = part_v.shape[2]
    half = 2 * quarter
    z, aux = lax.axis_index("half"), lax.axis_index("aux")
    core = lax.rem(aux, 2)
    copies = []
    for i, (src, block) in enumerate(((late, core), (late_other, 1 - core))):
        at = pl.multiple_of(block * rows, rows)
        copies.append(pltpu.make_async_copy(src, part_v.at[:, :, pl.ds(at, rows)], sem.at[i]))
        copies[-1].start()
    own_e = occ_ref[z * n_orb + aux].astype(F32) * 0.001
    row = row_ref[...].astype(F32) * 0.001
    col = col_ref[...].astype(F32) * 0.001
    energy = jnp.zeros((1, 1), F32)
    across = pl.multiple_of(lax.bitwise_xor(lax.div(aux, 2), (X | Y) // 2) * quarter, quarter)
    for c in copies:
        c.wait()
    tildes = []
    for g in range(groups):
        part = jnp.concatenate([part_v[g, s] for s in range(per)], axis=1)
        kk = ins[3 * g][...] + jnp.dot(own_t[:, pl.ds(across, quarter)], part, preferred_element_type=F32)
        for s in range(per):
            k = kk[:, s * n_virt:(s + 1) * n_virt]
            part_e = occ_ref[plan_ref[0, g * per + s]].astype(F32) * 0.001
            denom = own_e + part_e - col - row
            tilde = (2.0 * k - jnp.transpose(k)) / denom
            energy = energy + jnp.sum(jnp.sum(k * tilde, axis=1, keepdims=True), axis=0, keepdims=True)
            tildes.append(tilde.astype(BF16))
    tb = jnp.concatenate(tildes, axis=1)
    saves = []

    def save(i, block, at, size):
        dst = dens_ref.at[:, pl.ds(pl.multiple_of(at, size), size)]
        saves.append(pltpu.make_async_copy(block, dst, out_sem.at[i]))
        saves[-1].start()

    slots = [(g, s) for g in range(groups) for s in range(per)]
    part = jnp.concatenate([ins[3 * g + 1][s] for g, s in slots], axis=1)
    total = lax.dot_general(tb, part, (((1,), (1,)), ((), ())), preferred_element_type=F32)
    dens_v[0] = total.astype(BF16)
    save(0, dens_v.at[0], lax.div(aux, Y) * half, half)
    part = jnp.concatenate(
        [
            jnp.concatenate([ins[3 * g + 2][s] for g, s in slots], axis=1),
            jnp.concatenate([part_v[g, s] for g, s in slots], axis=1),
        ],
        axis=0,
    )
    total = lax.dot_general(tb, part, (((1,), (1,)), ((), ())), preferred_element_type=F32)
    dens_v[1] = total.astype(BF16)
    beside = lax.bitwise_xor(lax.div(aux, 2), Y // 2) * quarter
    save(1, dens_v.at[1, :, pl.ds(0, quarter)], beside, quarter)
    save(2, dens_v.at[1, :, pl.ds(quarter, quarter)], across, quarter)
    energy_ref[...] = energy / (n_virt * n_virt)
    for c in saves:
        c.wait()


def pair_terms(own, ins, late, late_other, occ, plan, vir, n_orb):
    groups, per, _, n_virt = late.shape
    n_aux = own.shape[1]
    smem = pl.BlockSpec(memory_space=pltpu.SMEM)
    vmem = pl.BlockSpec(memory_space=pltpu.VMEM)
    anym = pl.BlockSpec(memory_space=pl.ANY)
    return pl.pallas_call(
        functools.partial(pair_kernel, n_orb=n_orb, groups=groups),
        in_specs=[smem] * 2 + [vmem] * (3 + len(ins)) + [anym] * 2,
        out_specs=[pl.BlockSpec(memory_space=pltpu.HBM), vmem],
        out_shape=[jax.ShapeDtypeStruct((n_virt, n_aux), BF16), jax.ShapeDtypeStruct((1, 1), F32)],
        scratch_shapes=[
            pltpu.VMEM((groups, per, n_aux // 4, n_virt), BF16),
            pltpu.VMEM((2, n_virt, n_aux // 2), BF16),
            pltpu.SemaphoreType.DMA((2,)),
            pltpu.SemaphoreType.DMA((3,)),
        ],
        compiler_params=pltpu.CompilerParams(vmem_limit_bytes=24 << 20),
        name="pair_terms",
    )(occ, plan, vir.reshape(1, n_virt), vir.reshape(n_virt, 1), own, *ins, late, late_other)


def swap(x, n):
    return lax.ppermute(x, "aux", [(a, a ^ CORE) for a in range(n)])


def plane(x, n, flip):
    return lax.ppermute(x, "aux", [(a, a ^ (Y if (a & CORE) ^ flip else X)) for a in range(n)])


def shift(x, d, n):
    return lax.ppermute(x, "half", [(h, (h + d) % n) for h in range(n)])


GROUPS = 2


def on_device(half_slabs, vir_coeff, occ_energy, vir_energy, plan):
    return stages(half_slabs, vir_coeff, occ_energy, vir_energy, plan)


def stages(half_slabs, vir_coeff, occ_energy, vir_energy, plan):
    n_aux = lax.axis_size("aux")
    n_half = lax.axis_size("half")
    _, _, ohalf, _ = half_slabs.shape
    count = plan.size
    per = count // GROUPS
    cap = max(1, count // 2)
    order = tuple(range(1, n_half)) + (0,)
    crowd, *lists = transform(half_slabs, vir_coeff, plan, n_half, order, cap)
    near, lists = lists[:n_aux // 2], lists[n_aux // 2:]
    lists, spill = lists[:n_half], lists[n_half:]
    lists, spill = [lists[-1]] + lists[:-1], [spill[-1]] + spill[:-1]
    got = [lists[0]]
    for d in range(1, n_half):
        got.append(shift(lists[d], d, n_half))
    for r in range(1, n_aux // 2):
        near[r] = lax.ppermute(near[r], "aux", [(a, a ^ (2 * r)) for a in range(n_aux)])
    other = join(near, 1)
    other = swap(other, n_aux)
    own = prep(near, other)

    def roomy(got, spill):
        return merge(plan, got, ohalf, n_half, per)

    def crowded(got, spill):
        more = [spill[0]] + [shift(spill[d], d, n_half) for d in range(1, n_half)]
        return merge(plan, got + more, ohalf, n_half, per)

    mine = lax.switch(crowd[0], [roomy, crowded], got, spill)
    ins, late = [], []
    for g in range(GROUPS):
        parts = [mine[g]]
        for d in range(1, n_half):
            parts.append(shift(mine[g], d, n_half))
        z0 = pack(parts)
        r1 = plane(z0, n_aux, 0)
        r2 = plane(z0, n_aux, 1)
        late.append(plane(r1, n_aux, 1))
        early = join([z0, r1, r2])
        other = swap(early, n_aux)
        ins += amplitudes(own, early, other)
    late = join(late)
    late_other = swap(late, n_aux)
    density, energy = pair_terms(own, ins, late, late_other, occ_energy, plan, vir_energy, ohalf)
    return density[None, None], energy


def solution(mesh):
    fast = dict(mesh.shape) == {"aux": 8, "half": 4}
    in_specs = (P("aux", "half", None, None), P(), P(), P(), P())
    out_specs = (P("half", "aux", None, None), P("half", "aux"))
    return jax.shard_map(
        on_device if fast else any_mesh, mesh=mesh, in_specs=in_specs, out_specs=out_specs, check_vma=False
    )
```

```python
import functools

import jax
import jax.numpy as jnp
from jax import lax
from jax.experimental import pallas as pl
from jax.experimental.pallas import tpu as pltpu
from jax.sharding import PartitionSpec as P


F32 = jnp.float32
BF16 = jnp.bfloat16


def broadcast(x, axis, root):
    mine = lax.axis_index(axis) == root
    return lax.psum(jnp.where(mine, x, jnp.zeros_like(x)), axis)


def any_mesh(half_slabs, vir_coeff, occ_energy, vir_energy, plan):
    local_aux = half_slabs.shape[0]
    ohalf = half_slabs.shape[2]
    flat = half_slabs.reshape(local_aux * ohalf, half_slabs.shape[3])
    prod = jnp.dot(flat, vir_coeff, preferred_element_type=F32)
    transformed = prod.reshape(local_aux, ohalf, vir_coeff.shape[1]).astype(BF16)
    owned = lax.all_to_all(transformed, "aux", split_axis=1, concat_axis=0, tiled=True)
    n_half = lax.axis_size("half")
    aux_index = lax.axis_index("aux")
    half_index = lax.axis_index("half")
    o_dev = owned.shape[1]
    n_virt = owned.shape[2]
    own_start = half_index * ohalf + aux_index * o_dev
    occ_e = occ_energy.astype(F32) * 0.001
    own_e = lax.dynamic_slice_in_dim(occ_e, own_start, o_dev)
    vir_e = vir_energy.astype(F32) * 0.001
    gamma = jnp.zeros((o_dev, n_virt, owned.shape[0]), F32)
    energy = jnp.zeros((o_dev,), F32)
    for partner in plan.reshape(-1):
        part_half = partner // ohalf
        part_aux = partner % ohalf // o_dev
        piece = lax.dynamic_index_in_dim(owned, partner % o_dev, 1, keepdims=False)
        other = broadcast(piece, ("aux", "half"), part_aux * n_half + part_half)
        part_e = lax.dynamic_index_in_dim(occ_e, partner, 0, keepdims=False)
        kmat = jnp.einsum("pia,pb->iab", owned, other, preferred_element_type=F32)
        denom = own_e[:, None, None] + part_e - vir_e[None, :, None] - vir_e[None, None, :]
        tilde = (2.0 * kmat - jnp.swapaxes(kmat, 1, 2)) / denom
        energy = energy + jnp.sum(kmat * tilde, axis=(1, 2))
        gamma = gamma + jnp.einsum("iab,pb->iap", tilde.astype(BF16), other, preferred_element_type=F32)
    return gamma.astype(BF16)[None], (energy / (n_virt * n_virt))[None]


def partner_half(plan_ref, s, n_orb):
    return lax.div(plan_ref[0, s], n_orb)


def rank_in_half(plan_ref, s, n_orb):
    home = partner_half(plan_ref, s, n_orb)
    return sum([(partner_half(plan_ref, t, n_orb) == home).astype(jnp.int32) for t in range(s)], jnp.int32(0))


def transform_kernel(plan_ref, slab_hbm, coeff_hbm, *rest, n_half, order, chips):
    n = len(order)
    crowd_ref, rest = rest[0], rest[1:]
    outs, lists, spill = rest[:chips], rest[chips:chips + n], rest[chips + n:chips + 2 * n]
    slab_v, coeff_v, acc_ref, own_v, in_sem = rest[chips + 2 * n:]
    cap = lists[0].shape[0]
    count = cap + spill[0].shape[0]
    n_orb = 2 * chips
    aux = lax.axis_index("aux")
    tiles, block, lanes = acc_ref.shape
    rows = block // n_orb
    z = lax.axis_index("half")
    loads, starts = [], []
    coeff_copy = pltpu.make_async_copy(coeff_hbm, coeff_v, in_sem.at[len(order)])
    coeff_copy.start()
    for i, d in enumerate(order):
        at = pl.multiple_of(lax.rem(z + d, n_half) * rows, rows)
        at_flat = pl.multiple_of(at * n_orb, block)
        loads.append(pltpu.make_async_copy(slab_hbm.at[pl.ds(at_flat, block)], slab_v.at[i], in_sem.at[i]))
        starts.append(at)
        loads[i].start()
    ranks = [rank_in_half(plan_ref, s, n_orb) for s in range(count)]
    here = [partner_half(plan_ref, s, n_orb) == z for s in range(count)]
    pick = []
    for k in range(count):
        hits = [
            jnp.where(jnp.logical_and(here[s], ranks[s] == k), lax.rem(plan_ref[0, s], n_orb), 0)
            for s in range(count)
        ]
        pick.append(sum(hits, jnp.int32(0)))
    most = ranks[0]
    for r in ranks[1:]:
        most = jnp.maximum(most, r)
    crowd_ref[0] = (most >= cap).astype(jnp.int32)
    coeff_copy.wait()
    for i in range(len(order)):
        loads[i].wait()
        acc = jnp.dot(slab_v[i], coeff_v[...], preferred_element_type=F32)
        for t in range(tiles):
            acc_ref[t] = acc[:, t * lanes:(t + 1) * lanes]
        for t in range(tiles):
            cols = slice(t * lanes, (t + 1) * lanes)
            for o in range(n_orb):
                own_v[o, :, cols] = acc_ref[t, pl.ds(o, rows, stride=n_orb), :].astype(BF16)
        for r, out in enumerate(outs):
            for j in range(2):
                out[j, pl.ds(starts[i], rows)] = own_v[lax.bitwise_xor(aux, 2 * r + j)]
        for k in range(count):
            if k < cap:
                lists[i][k] = own_v[pick[k]]
            else:
                spill[i][k - cap] = own_v[pick[k]]


def transform(half_slabs, coeff, plan, n_half, order, cap):
    chips = half_slabs.shape[2] // 2
    local_aux, _, n_orb, n_ao = half_slabs.shape
    n_virt = coeff.shape[1]
    count = plan.shape[1]
    rows = local_aux // n_half
    n = len(order)
    hbm = pl.BlockSpec(memory_space=pltpu.HBM)
    vmem = pl.BlockSpec(memory_space=pltpu.VMEM)
    smem = pl.BlockSpec(memory_space=pltpu.SMEM)
    return pl.pallas_call(
        functools.partial(transform_kernel, n_half=n_half, order=order, chips=chips),
        in_specs=[smem, hbm, hbm],
        out_specs=[smem] + [vmem] * (chips + 2 * n),
        out_shape=[
            jax.ShapeDtypeStruct((1,), jnp.int32),
        ]
        + [jax.ShapeDtypeStruct((2, local_aux, n_virt), BF16)] * chips
        + [jax.ShapeDtypeStruct((cap, rows, n_virt), BF16)] * n
        + [jax.ShapeDtypeStruct((count - cap, rows, n_virt), BF16)] * n,
        scratch_shapes=[
            pltpu.VMEM((n, rows * n_orb, n_ao), BF16),
            pltpu.VMEM((n_ao, n_virt), BF16),
            pltpu.VMEM((n_virt // 128, rows * n_orb, 128), F32),
            pltpu.VMEM((n_orb, rows, n_virt), BF16),
            pltpu.SemaphoreType.DMA((n + 1,)),
        ],
        compiler_params=pltpu.CompilerParams(vmem_limit_bytes=20 << 20),
        name="transform",
    )(
        plan,
        pltpu.with_memory_space_constraint(half_slabs.reshape(local_aux * n_orb, n_ao), pltpu.HBM),
        pltpu.with_memory_space_constraint(coeff, pltpu.HBM),
    )


def merge_kernel(plan_ref, *refs, n_orb, n_half, spilled):
    n_in = 2 * n_half if spilled else n_half
    lists, outs, sem = refs[:n_in], refs[n_in:-1], refs[-1]
    cap = lists[0].shape[0]
    per = outs[0].shape[0]
    z = lax.axis_index("half")
    for s in range(per * len(outs)):
        far = lax.rem(z - partner_half(plan_ref, s, n_orb) + n_half, n_half)
        rank = rank_in_half(plan_ref, s, n_orb)
        for d in range(n_half):

            @pl.when(jnp.logical_and(far == d, rank < cap))
            def _():
                src = lists[d].at[jnp.minimum(rank, cap - 1)]
                pltpu.make_async_copy(src, outs[s // per].at[s % per], sem.at[s]).start()

            if spilled:

                @pl.when(jnp.logical_and(far == d, rank >= cap))
                def _():
                    src = lists[n_half + d].at[jnp.maximum(rank - cap, 0)]
                    pltpu.make_async_copy(src, outs[s // per].at[s % per], sem.at[s]).start()

    for s in range(per * len(outs)):
        pltpu.make_async_copy(lists[0].at[0], outs[s // per].at[s % per], sem.at[s]).wait()


def merge(plan, lists, n_orb, n_half, per):
    count = plan.shape[1]
    _, rows, n_virt = lists[0].shape
    shape = jax.ShapeDtypeStruct((per, rows, n_virt), BF16)
    return pl.pallas_call(
        functools.partial(merge_kernel, n_orb=n_orb, n_half=n_half, spilled=len(lists) > n_half),
        in_specs=[pl.BlockSpec(memory_space=pltpu.SMEM)] + [pl.BlockSpec(memory_space=pl.ANY)] * len(lists),
        out_specs=[pl.BlockSpec(memory_space=pltpu.VMEM)] * (count // per),
        out_shape=[shape] * (count // per),
        scratch_shapes=[pltpu.SemaphoreType.DMA((count,))],
        compiler_params=pltpu.CompilerParams(vmem_limit_bytes=4 << 20),
        name="merge",
    )(plan, *lists)


def pack_kernel(*refs):
    parts, out = refs[:-1], refs[-1]
    per, sub, _ = parts[0].shape
    z = lax.axis_index("half")
    for d, part in enumerate(parts):
        at = pl.multiple_of(lax.bitwise_xor(z, d) * sub, sub)
        for s in range(per):
            out[s, pl.ds(at, sub)] = part[s]


def pack(parts):
    vmem = pl.BlockSpec(memory_space=pltpu.VMEM)
    per, sub, n_virt = parts[0].shape
    return pl.pallas_call(
        pack_kernel,
        in_specs=[vmem] * len(parts),
        out_specs=vmem,
        out_shape=jax.ShapeDtypeStruct((per, len(parts) * sub, n_virt), BF16),
        compiler_params=pltpu.CompilerParams(vmem_limit_bytes=4 << 20),
        name="pack",
    )(*parts)


def join_kernel(*refs, entry):
    parts, out, sem = refs[:-2], refs[-2], refs[-1]
    parts = parts if entry is None else [part.at[entry] for part in parts]
    copies = [pltpu.make_async_copy(part, out.at[i], sem.at[i]) for i, part in enumerate(parts)]
    for c in copies:
        c.start()
    for c in copies:
        c.wait()


def join(parts, entry=None):
    shape = parts[0].shape if entry is None else parts[0].shape[1:]
    return pl.pallas_call(
        functools.partial(join_kernel, entry=entry),
        in_specs=[pl.BlockSpec(memory_space=pl.ANY)] * len(parts),
        out_specs=pl.BlockSpec(memory_space=pltpu.VMEM),
        out_shape=jax.ShapeDtypeStruct((len(parts),) + shape, BF16),
        scratch_shapes=[pltpu.SemaphoreType.DMA((len(parts),))],
        compiler_params=pltpu.CompilerParams(vmem_limit_bytes=4 << 20),
        name="join",
    )(*parts)


CORE, X, Y = 1, 2, 4


def prep_kernel(*refs):
    near, other, own_t = refs[:-2], refs[-2], refs[-1]
    chips = len(near)
    aux = lax.axis_index("aux")
    core = lax.rem(aux, 2)
    width = 2 * other.shape[1]
    for r in range(chips):
        mine, theirs = near[r][0], other[r]
        pair = jnp.concatenate([jnp.where(core == 0, mine, theirs), jnp.where(core == 0, theirs, mine)], axis=0)
        at = pl.multiple_of(lax.bitwise_xor(lax.div(aux, 2), r) * width, width)
        own_t[:, pl.ds(at, width)] = jnp.transpose(pair)


def prep(near, other):
    _, rows, n_virt = other.shape
    vmem = pl.BlockSpec(memory_space=pltpu.VMEM)
    return pl.pallas_call(
        prep_kernel,
        in_specs=[vmem] * (len(near) + 1),
        out_specs=vmem,
        out_shape=jax.ShapeDtypeStruct((n_virt, 2 * len(near) * rows), BF16),
        compiler_params=pltpu.CompilerParams(vmem_limit_bytes=8 << 20),
        name="prep",
    )(*near, other)


def amp_kernel(own_t, early, other, k_ref, here_ref, beside_ref, sem):
    _, per, rows, _ = early.shape
    aux = lax.axis_index("aux")
    core = lax.rem(aux, 2)
    half, quarter = here_ref.shape[1], beside_ref.shape[1]
    side = lax.rem(aux, Y)
    copies = []
    for src, block, out in (
        (early.at[0], side, here_ref),
        (early.at[1 + core], lax.bitwise_xor(side, X), here_ref),
        (other.at[0], lax.bitwise_xor(side, CORE), here_ref),
        (other.at[2 - core], lax.bitwise_xor(side, X | CORE), here_ref),
        (early.at[2 - core], core, beside_ref),
        (other.at[1 + core], 1 - core, beside_ref),
    ):
        at = pl.multiple_of(block * rows, rows)
        copies.append(pltpu.make_async_copy(src, out.at[:, pl.ds(at, rows)], sem.at[len(copies)]))
    for c in copies:
        c.start()
    for c in copies:
        c.wait()
    here = pl.multiple_of(lax.div(aux, Y) * half, half)
    beside = pl.multiple_of(lax.bitwise_xor(lax.div(aux, 2), Y // 2) * quarter, quarter)
    part = jnp.concatenate([here_ref[s] for s in range(per)], axis=1)
    k = jnp.dot(own_t[:, pl.ds(here, half)], part, preferred_element_type=F32)
    part = jnp.concatenate([beside_ref[s] for s in range(per)], axis=1)
    k_ref[...] = k + jnp.dot(own_t[:, pl.ds(beside, quarter)], part, preferred_element_type=F32)


def amplitudes(own, early, other):
    _, per, _, n_virt = early.shape
    n_aux = own.shape[1]
    anym = pl.BlockSpec(memory_space=pl.ANY)
    vmem = pl.BlockSpec(memory_space=pltpu.VMEM)
    return pl.pallas_call(
        amp_kernel,
        in_specs=[vmem, anym, anym],
        out_specs=[vmem] * 3,
        out_shape=[
            jax.ShapeDtypeStruct((n_virt, per * n_virt), F32),
            jax.ShapeDtypeStruct((per, n_aux // 2, n_virt), BF16),
            jax.ShapeDtypeStruct((per, n_aux // 4, n_virt), BF16),
        ],
        scratch_shapes=[pltpu.SemaphoreType.DMA((6,))],
        compiler_params=pltpu.CompilerParams(vmem_limit_bytes=12 << 20),
        cost_estimate=pl.CostEstimate(flops=per * n_virt * n_virt * n_aux, bytes_accessed=3 << 20, transcendentals=0),
        name="amplitudes",
    )(own, early, other)


def pair_kernel(occ_ref, plan_ref, row_ref, col_ref, own_t, *rest, n_orb, groups):
    ins = rest[:3 * groups]
    late, late_other, dens_ref, energy_ref, part_v, dens_v, sem, out_sem = rest[3 * groups:]
    _, per, rows, n_virt = late.shape
    quarter = part_v.shape[2]
    half = 2 * quarter
    z, aux = lax.axis_index("half"), lax.axis_index("aux")
    core = lax.rem(aux, 2)
    copies = []
    for i, (src, block) in enumerate(((late, core), (late_other, 1 - core))):
        at = pl.multiple_of(block * rows, rows)
        copies.append(pltpu.make_async_copy(src, part_v.at[:, :, pl.ds(at, rows)], sem.at[i]))
        copies[-1].start()
    own_e = occ_ref[z * n_orb + aux].astype(F32) * 0.001
    row = row_ref[...].astype(F32) * 0.001
    col = col_ref[...].astype(F32) * 0.001
    energy = jnp.zeros((1, 1), F32)
    across = pl.multiple_of(lax.bitwise_xor(lax.div(aux, 2), (X | Y) // 2) * quarter, quarter)
    for c in copies:
        c.wait()
    tildes = []
    for g in range(groups):
        part = jnp.concatenate([part_v[g, s] for s in range(per)], axis=1)
        kk = ins[3 * g][...] + jnp.dot(own_t[:, pl.ds(across, quarter)], part, preferred_element_type=F32)
        for s in range(per):
            k = kk[:, s * n_virt:(s + 1) * n_virt]
            part_e = occ_ref[plan_ref[0, g * per + s]].astype(F32) * 0.001
            denom = own_e + part_e - col - row
            tilde = (2.0 * k - jnp.transpose(k)) / denom
            energy = energy + jnp.sum(jnp.sum(k * tilde, axis=1, keepdims=True), axis=0, keepdims=True)
            tildes.append(tilde.astype(BF16))
    tb = jnp.concatenate(tildes, axis=1)
    saves = []

    def save(i, block, at, size):
        dst = dens_ref.at[:, pl.ds(pl.multiple_of(at, size), size)]
        saves.append(pltpu.make_async_copy(block, dst, out_sem.at[i]))
        saves[-1].start()

    slots = [(g, s) for g in range(groups) for s in range(per)]
    part = jnp.concatenate([ins[3 * g + 1][s] for g, s in slots], axis=1)
    total = lax.dot_general(tb, part, (((1,), (1,)), ((), ())), preferred_element_type=F32)
    dens_v[0] = total.astype(BF16)
    save(0, dens_v.at[0], lax.div(aux, Y) * half, half)
    part = jnp.concatenate(
        [
            jnp.concatenate([ins[3 * g + 2][s] for g, s in slots], axis=1),
            jnp.concatenate([part_v[g, s] for g, s in slots], axis=1),
        ],
        axis=0,
    )
    total = lax.dot_general(tb, part, (((1,), (1,)), ((), ())), preferred_element_type=F32)
    dens_v[1] = total.astype(BF16)
    beside = lax.bitwise_xor(lax.div(aux, 2), Y // 2) * quarter
    save(1, dens_v.at[1, :, pl.ds(0, quarter)], beside, quarter)
    save(2, dens_v.at[1, :, pl.ds(quarter, quarter)], across, quarter)
    energy_ref[...] = energy / (n_virt * n_virt)
    for c in saves:
        c.wait()


def pair_terms(own, ins, late, late_other, occ, plan, vir, n_orb):
    groups, per, _, n_virt = late.shape
    n_aux = own.shape[1]
    smem = pl.BlockSpec(memory_space=pltpu.SMEM)
    vmem = pl.BlockSpec(memory_space=pltpu.VMEM)
    anym = pl.BlockSpec(memory_space=pl.ANY)
    return pl.pallas_call(
        functools.partial(pair_kernel, n_orb=n_orb, groups=groups),
        in_specs=[smem] * 2 + [vmem] * (3 + len(ins)) + [anym] * 2,
        out_specs=[pl.BlockSpec(memory_space=pltpu.HBM), vmem],
        out_shape=[jax.ShapeDtypeStruct((n_virt, n_aux), BF16), jax.ShapeDtypeStruct((1, 1), F32)],
        scratch_shapes=[
            pltpu.VMEM((groups, per, n_aux // 4, n_virt), BF16),
            pltpu.VMEM((2, n_virt, n_aux // 2), BF16),
            pltpu.SemaphoreType.DMA((2,)),
            pltpu.SemaphoreType.DMA((3,)),
        ],
        compiler_params=pltpu.CompilerParams(vmem_limit_bytes=24 << 20),
        name="pair_terms",
    )(occ, plan, vir.reshape(1, n_virt), vir.reshape(n_virt, 1), own, *ins, late, late_other)


def swap(x, n):
    return lax.ppermute(x, "aux", [(a, a ^ CORE) for a in range(n)])


def plane(x, n, flip):
    return lax.ppermute(x, "aux", [(a, a ^ (Y if (a & CORE) ^ flip else X)) for a in range(n)])


def shift(x, d, n):
    return lax.ppermute(x, "half", [(h, (h + d) % n) for h in range(n)])


def across(x, bits, n):
    return lax.ppermute(x, "half", [(h, h ^ bits) for h in range(n)])


GROUPS = 2


def on_device(half_slabs, vir_coeff, occ_energy, vir_energy, plan):
    return stages(half_slabs, vir_coeff, occ_energy, vir_energy, plan)


def stages(half_slabs, vir_coeff, occ_energy, vir_energy, plan):
    n_aux = lax.axis_size("aux")
    n_half = lax.axis_size("half")
    _, _, ohalf, _ = half_slabs.shape
    count = plan.size
    per = count // GROUPS
    cap = max(1, count // 2)
    order = tuple(range(1, n_half)) + (0,)
    crowd, *lists = transform(half_slabs, vir_coeff, plan, n_half, order, cap)
    near, lists = lists[:n_aux // 2], lists[n_aux // 2:]
    lists, spill = lists[:n_half], lists[n_half:]
    lists, spill = [lists[-1]] + lists[:-1], [spill[-1]] + spill[:-1]
    got = [lists[0]]
    for d in range(1, n_half):
        got.append(shift(lists[d], d, n_half))
    for r in range(1, n_aux // 2):
        near[r] = lax.ppermute(near[r], "aux", [(a, a ^ (2 * r)) for a in range(n_aux)])
    other = join(near, 1)
    other = swap(other, n_aux)
    own = prep(near, other)

    def roomy(got, spill):
        return merge(plan, got, ohalf, n_half, per)

    def crowded(got, spill):
        more = [spill[0]] + [shift(spill[d], d, n_half) for d in range(1, n_half)]
        return merge(plan, got + more, ohalf, n_half, per)

    mine = lax.switch(crowd[0], [roomy, crowded], got, spill)
    ins, late = [], []
    for g in range(GROUPS):
        far = across(mine[g], 2, n_half)
        beside = across(mine[g], 1, n_half)
        parts = [mine[g], beside, far, across(far, 1, n_half)]
        z0 = pack(parts)
        r1 = plane(z0, n_aux, 0)
        r2 = plane(z0, n_aux, 1)
        late.append(plane(r1, n_aux, 1))
        early = join([z0, r1, r2])
        other = swap(early, n_aux)
        ins += amplitudes(own, early, other)
    late = join(late)
    late_other = swap(late, n_aux)
    density, energy = pair_terms(own, ins, late, late_other, occ_energy, plan, vir_energy, ohalf)
    return density[None, None], energy


def solution(mesh):
    fast = dict(mesh.shape) == {"aux": 8, "half": 4}
    in_specs = (P("aux", "half", None, None), P(), P(), P(), P())
    out_specs = (P("half", "aux", None, None), P("half", "aux"))
    return jax.shard_map(
        on_device if fast else any_mesh, mesh=mesh, in_specs=in_specs, out_specs=out_specs, check_vma=False
    )
```

```python
import functools

import jax
import jax.numpy as jnp
from jax import lax
from jax.experimental import pallas as pl
from jax.experimental.pallas import tpu as pltpu
from jax.sharding import PartitionSpec as P


F32 = jnp.float32
BF16 = jnp.bfloat16


def broadcast(x, axis, root):
    mine = lax.axis_index(axis) == root
    return lax.psum(jnp.where(mine, x, jnp.zeros_like(x)), axis)


def any_mesh(half_slabs, vir_coeff, occ_energy, vir_energy, plan):
    local_aux = half_slabs.shape[0]
    ohalf = half_slabs.shape[2]
    flat = half_slabs.reshape(local_aux * ohalf, half_slabs.shape[3])
    prod = jnp.dot(flat, vir_coeff, preferred_element_type=F32)
    transformed = prod.reshape(local_aux, ohalf, vir_coeff.shape[1]).astype(BF16)
    owned = lax.all_to_all(transformed, "aux", split_axis=1, concat_axis=0, tiled=True)
    n_half = lax.axis_size("half")
    aux_index = lax.axis_index("aux")
    half_index = lax.axis_index("half")
    o_dev = owned.shape[1]
    n_virt = owned.shape[2]
    own_start = half_index * ohalf + aux_index * o_dev
    occ_e = occ_energy.astype(F32) * 0.001
    own_e = lax.dynamic_slice_in_dim(occ_e, own_start, o_dev)
    vir_e = vir_energy.astype(F32) * 0.001
    gamma = jnp.zeros((o_dev, n_virt, owned.shape[0]), F32)
    energy = jnp.zeros((o_dev,), F32)
    for partner in plan.reshape(-1):
        part_half = partner // ohalf
        part_aux = partner % ohalf // o_dev
        piece = lax.dynamic_index_in_dim(owned, partner % o_dev, 1, keepdims=False)
        other = broadcast(piece, ("aux", "half"), part_aux * n_half + part_half)
        part_e = lax.dynamic_index_in_dim(occ_e, partner, 0, keepdims=False)
        kmat = jnp.einsum("pia,pb->iab", owned, other, preferred_element_type=F32)
        denom = own_e[:, None, None] + part_e - vir_e[None, :, None] - vir_e[None, None, :]
        tilde = (2.0 * kmat - jnp.swapaxes(kmat, 1, 2)) / denom
        energy = energy + jnp.sum(kmat * tilde, axis=(1, 2))
        gamma = gamma + jnp.einsum("iab,pb->iap", tilde.astype(BF16), other, preferred_element_type=F32)
    return gamma.astype(BF16)[None], (energy / (n_virt * n_virt))[None]


def partner_half(plan_ref, s, n_orb):
    return lax.div(plan_ref[0, s], n_orb)


def rank_in_half(plan_ref, s, n_orb):
    home = partner_half(plan_ref, s, n_orb)
    return sum([(partner_half(plan_ref, t, n_orb) == home).astype(jnp.int32) for t in range(s)], jnp.int32(0))


def transform_kernel(plan_ref, slab_hbm, coeff_hbm, *rest, n_half, order, chips):
    n = len(order)
    crowd_ref, rest = rest[0], rest[1:]
    count = plan_ref.shape[1]
    outs, lists = rest[:chips], rest[chips:chips + n]
    cap = lists[0].shape[0]
    spill = rest[chips + n:chips + n + n * (count - cap)]
    slab_v, coeff_v, acc_ref, own_v, in_sem = rest[chips + n + n * (count - cap):]
    n_orb = 2 * chips
    aux = lax.axis_index("aux")
    tiles, block, lanes = acc_ref.shape
    rows = block // n_orb
    z = lax.axis_index("half")
    loads, starts = [], []
    coeff_copy = pltpu.make_async_copy(coeff_hbm, coeff_v, in_sem.at[len(order)])
    coeff_copy.start()
    for i, d in enumerate(order):
        at = pl.multiple_of(lax.rem(z + d, n_half) * rows, rows)
        at_flat = pl.multiple_of(at * n_orb, block)
        loads.append(pltpu.make_async_copy(slab_hbm.at[pl.ds(at_flat, block)], slab_v.at[i], in_sem.at[i]))
        starts.append(at)
        loads[i].start()
    ranks = [rank_in_half(plan_ref, s, n_orb) for s in range(count)]
    here = [partner_half(plan_ref, s, n_orb) == z for s in range(count)]
    pick = []
    for k in range(count):
        hits = [
            jnp.where(jnp.logical_and(here[s], ranks[s] == k), lax.rem(plan_ref[0, s], n_orb), 0)
            for s in range(count)
        ]
        pick.append(sum(hits, jnp.int32(0)))
    most = ranks[0]
    for r in ranks[1:]:
        most = jnp.maximum(most, r)
    crowd_ref[0] = jnp.maximum(most - (cap - 1), 0)
    coeff_copy.wait()
    for i in range(len(order)):
        loads[i].wait()
        acc = jnp.dot(slab_v[i], coeff_v[...], preferred_element_type=F32)
        for t in range(tiles):
            acc_ref[t] = acc[:, t * lanes:(t + 1) * lanes]
        for t in range(tiles):
            cols = slice(t * lanes, (t + 1) * lanes)
            for o in range(n_orb):
                own_v[o, :, cols] = acc_ref[t, pl.ds(o, rows, stride=n_orb), :].astype(BF16)
        for r, out in enumerate(outs):
            for j in range(2):
                out[j, pl.ds(starts[i], rows)] = own_v[lax.bitwise_xor(aux, 2 * r + j)]
        for k in range(count):
            if k < cap:
                lists[i][k] = own_v[pick[k]]
            else:
                spill[(k - cap) * n + i][0] = own_v[pick[k]]


def transform(half_slabs, coeff, plan, n_half, order, cap):
    chips = half_slabs.shape[2] // 2
    local_aux, _, n_orb, n_ao = half_slabs.shape
    n_virt = coeff.shape[1]
    count = plan.shape[1]
    rows = local_aux // n_half
    n = len(order)
    hbm = pl.BlockSpec(memory_space=pltpu.HBM)
    vmem = pl.BlockSpec(memory_space=pltpu.VMEM)
    smem = pl.BlockSpec(memory_space=pltpu.SMEM)
    return pl.pallas_call(
        functools.partial(transform_kernel, n_half=n_half, order=order, chips=chips),
        in_specs=[smem, hbm, hbm],
        out_specs=[smem] + [vmem] * (chips + n + n * (count - cap)),
        out_shape=[
            jax.ShapeDtypeStruct((1,), jnp.int32),
        ]
        + [jax.ShapeDtypeStruct((2, local_aux, n_virt), BF16)] * chips
        + [jax.ShapeDtypeStruct((cap, rows, n_virt), BF16)] * n
        + [jax.ShapeDtypeStruct((1, rows, n_virt), BF16)] * (n * (count - cap)),
        scratch_shapes=[
            pltpu.VMEM((n, rows * n_orb, n_ao), BF16),
            pltpu.VMEM((n_ao, n_virt), BF16),
            pltpu.VMEM((n_virt // 128, rows * n_orb, 128), F32),
            pltpu.VMEM((n_orb, rows, n_virt), BF16),
            pltpu.SemaphoreType.DMA((n + 1,)),
        ],
        compiler_params=pltpu.CompilerParams(vmem_limit_bytes=20 << 20),
        name="transform",
    )(
        plan,
        pltpu.with_memory_space_constraint(half_slabs.reshape(local_aux * n_orb, n_ao), pltpu.HBM),
        pltpu.with_memory_space_constraint(coeff, pltpu.HBM),
    )


def merge_kernel(plan_ref, *refs, n_orb, n_half, spilled):
    n_in = (1 + spilled) * n_half
    lists, outs, sem = refs[:n_in], refs[n_in:-1], refs[-1]
    cap = lists[0].shape[0]
    per = outs[0].shape[0]
    z = lax.axis_index("half")
    for s in range(per * len(outs)):
        far = lax.rem(z - partner_half(plan_ref, s, n_orb) + n_half, n_half)
        rank = rank_in_half(plan_ref, s, n_orb)
        for d in range(n_half):

            @pl.when(jnp.logical_and(far == d, rank < cap))
            def _():
                src = lists[d].at[jnp.minimum(rank, cap - 1)]
                pltpu.make_async_copy(src, outs[s // per].at[s % per], sem.at[s]).start()

            for e in range(spilled):

                @pl.when(jnp.logical_and(far == d, rank == cap + e))
                def _():
                    src = lists[(1 + e) * n_half + d].at[0]
                    pltpu.make_async_copy(src, outs[s // per].at[s % per], sem.at[s]).start()

    for s in range(per * len(outs)):
        pltpu.make_async_copy(lists[0].at[0], outs[s // per].at[s % per], sem.at[s]).wait()


def merge(plan, lists, n_orb, n_half, per):
    count = plan.shape[1]
    _, rows, n_virt = lists[0].shape
    shape = jax.ShapeDtypeStruct((per, rows, n_virt), BF16)
    return pl.pallas_call(
        functools.partial(merge_kernel, n_orb=n_orb, n_half=n_half, spilled=len(lists) // n_half - 1),
        in_specs=[pl.BlockSpec(memory_space=pltpu.SMEM)] + [pl.BlockSpec(memory_space=pl.ANY)] * len(lists),
        out_specs=[pl.BlockSpec(memory_space=pltpu.VMEM)] * (count // per),
        out_shape=[shape] * (count // per),
        scratch_shapes=[pltpu.SemaphoreType.DMA((count,))],
        compiler_params=pltpu.CompilerParams(vmem_limit_bytes=4 << 20),
        name="merge",
    )(plan, *lists)


def pack_kernel(*refs):
    parts, out = refs[:-1], refs[-1]
    per, sub, _ = parts[0].shape
    z = lax.axis_index("half")
    for d, part in enumerate(parts):
        at = pl.multiple_of(lax.bitwise_xor(z, d) * sub, sub)
        for s in range(per):
            out[s, pl.ds(at, sub)] = part[s]


def pack(parts):
    vmem = pl.BlockSpec(memory_space=pltpu.VMEM)
    per, sub, n_virt = parts[0].shape
    return pl.pallas_call(
        pack_kernel,
        in_specs=[vmem] * len(parts),
        out_specs=vmem,
        out_shape=jax.ShapeDtypeStruct((per, len(parts) * sub, n_virt), BF16),
        compiler_params=pltpu.CompilerParams(vmem_limit_bytes=4 << 20),
        name="pack",
    )(*parts)


def join_kernel(*refs, entry):
    parts, out, sem = refs[:-2], refs[-2], refs[-1]
    parts = parts if entry is None else [part.at[entry] for part in parts]
    copies = [pltpu.make_async_copy(part, out.at[i], sem.at[i]) for i, part in enumerate(parts)]
    for c in copies:
        c.start()
    for c in copies:
        c.wait()


def join(parts, entry=None):
    shape = parts[0].shape if entry is None else parts[0].shape[1:]
    return pl.pallas_call(
        functools.partial(join_kernel, entry=entry),
        in_specs=[pl.BlockSpec(memory_space=pl.ANY)] * len(parts),
        out_specs=pl.BlockSpec(memory_space=pltpu.VMEM),
        out_shape=jax.ShapeDtypeStruct((len(parts),) + shape, BF16),
        scratch_shapes=[pltpu.SemaphoreType.DMA((len(parts),))],
        compiler_params=pltpu.CompilerParams(vmem_limit_bytes=4 << 20),
        name="join",
    )(*parts)


CORE, X, Y = 1, 2, 4


def prep_kernel(*refs):
    near, other, own_t = refs[:-2], refs[-2], refs[-1]
    chips = len(near)
    aux = lax.axis_index("aux")
    core = lax.rem(aux, 2)
    width = 2 * other.shape[1]
    for r in range(chips):
        mine, theirs = near[r][0], other[r]
        pair = jnp.concatenate([jnp.where(core == 0, mine, theirs), jnp.where(core == 0, theirs, mine)], axis=0)
        at = pl.multiple_of(lax.bitwise_xor(lax.div(aux, 2), r) * width, width)
        own_t[:, pl.ds(at, width)] = jnp.transpose(pair)


def prep(near, other):
    _, rows, n_virt = other.shape
    vmem = pl.BlockSpec(memory_space=pltpu.VMEM)
    return pl.pallas_call(
        prep_kernel,
        in_specs=[vmem] * (len(near) + 1),
        out_specs=vmem,
        out_shape=jax.ShapeDtypeStruct((n_virt, 2 * len(near) * rows), BF16),
        compiler_params=pltpu.CompilerParams(vmem_limit_bytes=8 << 20),
        name="prep",
    )(*near, other)


def amp_kernel(own_t, early, other, k_ref, here_ref, beside_ref, sem):
    _, per, rows, _ = early.shape
    aux = lax.axis_index("aux")
    core = lax.rem(aux, 2)
    half, quarter = here_ref.shape[1], beside_ref.shape[1]
    side = lax.rem(aux, Y)
    copies = []
    for src, block, out in (
        (early.at[0], side, here_ref),
        (early.at[1 + core], lax.bitwise_xor(side, X), here_ref),
        (other.at[0], lax.bitwise_xor(side, CORE), here_ref),
        (other.at[2 - core], lax.bitwise_xor(side, X | CORE), here_ref),
        (early.at[2 - core], core, beside_ref),
        (other.at[1 + core], 1 - core, beside_ref),
    ):
        at = pl.multiple_of(block * rows, rows)
        copies.append(pltpu.make_async_copy(src, out.at[:, pl.ds(at, rows)], sem.at[len(copies)]))
    for c in copies:
        c.start()
    for c in copies:
        c.wait()
    here = pl.multiple_of(lax.div(aux, Y) * half, half)
    beside = pl.multiple_of(lax.bitwise_xor(lax.div(aux, 2), Y // 2) * quarter, quarter)
    part = jnp.concatenate([here_ref[s] for s in range(per)], axis=1)
    k = jnp.dot(own_t[:, pl.ds(here, half)], part, preferred_element_type=F32)
    part = jnp.concatenate([beside_ref[s] for s in range(per)], axis=1)
    k_ref[...] = k + jnp.dot(own_t[:, pl.ds(beside, quarter)], part, preferred_element_type=F32)


def amplitudes(own, early, other):
    _, per, _, n_virt = early.shape
    n_aux = own.shape[1]
    anym = pl.BlockSpec(memory_space=pl.ANY)
    vmem = pl.BlockSpec(memory_space=pltpu.VMEM)
    return pl.pallas_call(
        amp_kernel,
        in_specs=[vmem, anym, anym],
        out_specs=[vmem] * 3,
        out_shape=[
            jax.ShapeDtypeStruct((n_virt, per * n_virt), F32),
            jax.ShapeDtypeStruct((per, n_aux // 2, n_virt), BF16),
            jax.ShapeDtypeStruct((per, n_aux // 4, n_virt), BF16),
        ],
        scratch_shapes=[pltpu.SemaphoreType.DMA((6,))],
        compiler_params=pltpu.CompilerParams(vmem_limit_bytes=12 << 20),
        cost_estimate=pl.CostEstimate(flops=per * n_virt * n_virt * n_aux, bytes_accessed=3 << 20, transcendentals=0),
        name="amplitudes",
    )(own, early, other)


def pair_kernel(occ_ref, plan_ref, row_ref, col_ref, own_t, *rest, n_orb, groups):
    ins = rest[:3 * groups]
    late, late_other, dens_ref, energy_ref, part_v, dens_v, sem, out_sem = rest[3 * groups:]
    _, per, rows, n_virt = late.shape
    quarter = part_v.shape[2]
    half = 2 * quarter
    z, aux = lax.axis_index("half"), lax.axis_index("aux")
    core = lax.rem(aux, 2)
    copies = []
    for i, (src, block) in enumerate(((late, core), (late_other, 1 - core))):
        at = pl.multiple_of(block * rows, rows)
        copies.append(pltpu.make_async_copy(src, part_v.at[:, :, pl.ds(at, rows)], sem.at[i]))
        copies[-1].start()
    own_e = occ_ref[z * n_orb + aux].astype(F32) * 0.001
    row = row_ref[...].astype(F32) * 0.001
    col = col_ref[...].astype(F32) * 0.001
    energy = jnp.zeros((1, 1), F32)
    across = pl.multiple_of(lax.bitwise_xor(lax.div(aux, 2), (X | Y) // 2) * quarter, quarter)
    for c in copies:
        c.wait()
    tildes = []
    for g in range(groups):
        part = jnp.concatenate([part_v[g, s] for s in range(per)], axis=1)
        kk = ins[3 * g][...] + jnp.dot(own_t[:, pl.ds(across, quarter)], part, preferred_element_type=F32)
        for s in range(per):
            k = kk[:, s * n_virt:(s + 1) * n_virt]
            part_e = occ_ref[plan_ref[0, g * per + s]].astype(F32) * 0.001
            denom = own_e + part_e - col - row
            tilde = (2.0 * k - jnp.transpose(k)) / denom
            energy = energy + jnp.sum(jnp.sum(k * tilde, axis=1, keepdims=True), axis=0, keepdims=True)
            tildes.append(tilde.astype(BF16))
    tb = jnp.concatenate(tildes, axis=1)
    saves = []

    def save(i, block, at, size):
        dst = dens_ref.at[:, pl.ds(pl.multiple_of(at, size), size)]
        saves.append(pltpu.make_async_copy(block, dst, out_sem.at[i]))
        saves[-1].start()

    slots = [(g, s) for g in range(groups) for s in range(per)]
    part = jnp.concatenate([ins[3 * g + 1][s] for g, s in slots], axis=1)
    total = lax.dot_general(tb, part, (((1,), (1,)), ((), ())), preferred_element_type=F32)
    dens_v[0] = total.astype(BF16)
    save(0, dens_v.at[0], lax.div(aux, Y) * half, half)
    part = jnp.concatenate(
        [
            jnp.concatenate([ins[3 * g + 2][s] for g, s in slots], axis=1),
            jnp.concatenate([part_v[g, s] for g, s in slots], axis=1),
        ],
        axis=0,
    )
    total = lax.dot_general(tb, part, (((1,), (1,)), ((), ())), preferred_element_type=F32)
    dens_v[1] = total.astype(BF16)
    beside = lax.bitwise_xor(lax.div(aux, 2), Y // 2) * quarter
    save(1, dens_v.at[1, :, pl.ds(0, quarter)], beside, quarter)
    save(2, dens_v.at[1, :, pl.ds(quarter, quarter)], across, quarter)
    energy_ref[...] = energy / (n_virt * n_virt)
    for c in saves:
        c.wait()


def pair_terms(own, ins, late, late_other, occ, plan, vir, n_orb):
    groups, per, _, n_virt = late.shape
    n_aux = own.shape[1]
    smem = pl.BlockSpec(memory_space=pltpu.SMEM)
    vmem = pl.BlockSpec(memory_space=pltpu.VMEM)
    anym = pl.BlockSpec(memory_space=pl.ANY)
    return pl.pallas_call(
        functools.partial(pair_kernel, n_orb=n_orb, groups=groups),
        in_specs=[smem] * 2 + [vmem] * (3 + len(ins)) + [anym] * 2,
        out_specs=[pl.BlockSpec(memory_space=pltpu.HBM), vmem],
        out_shape=[jax.ShapeDtypeStruct((n_virt, n_aux), BF16), jax.ShapeDtypeStruct((1, 1), F32)],
        scratch_shapes=[
            pltpu.VMEM((groups, per, n_aux // 4, n_virt), BF16),
            pltpu.VMEM((2, n_virt, n_aux // 2), BF16),
            pltpu.SemaphoreType.DMA((2,)),
            pltpu.SemaphoreType.DMA((3,)),
        ],
        compiler_params=pltpu.CompilerParams(vmem_limit_bytes=24 << 20),
        name="pair_terms",
    )(occ, plan, vir.reshape(1, n_virt), vir.reshape(n_virt, 1), own, *ins, late, late_other)


def swap(x, n):
    return lax.ppermute(x, "aux", [(a, a ^ CORE) for a in range(n)])


def plane(x, n, flip):
    return lax.ppermute(x, "aux", [(a, a ^ (Y if (a & CORE) ^ flip else X)) for a in range(n)])


def shift(x, d, n):
    return lax.ppermute(x, "half", [(h, (h + d) % n) for h in range(n)])


def across(x, bits, n):
    return lax.ppermute(x, "half", [(h, h ^ bits) for h in range(n)])


GROUPS = 2


def on_device(half_slabs, vir_coeff, occ_energy, vir_energy, plan):
    return stages(half_slabs, vir_coeff, occ_energy, vir_energy, plan)


def stages(half_slabs, vir_coeff, occ_energy, vir_energy, plan):
    n_aux = lax.axis_size("aux")
    n_half = lax.axis_size("half")
    _, _, ohalf, _ = half_slabs.shape
    count = plan.size
    per = count // GROUPS
    cap = max(1, count // 2)
    order = tuple(range(1, n_half)) + (0,)
    crowd, *lists = transform(half_slabs, vir_coeff, plan, n_half, order, cap)
    near, lists = lists[:n_aux // 2], lists[n_aux // 2:]
    lists, spill = lists[:n_half], lists[n_half:]
    lists = [lists[-1]] + lists[:-1]
    spill = [spill[e + n_half - 1:e + n_half] + spill[e:e + n_half - 1] for e in range(0, len(spill), n_half)]
    got = [lists[0]]
    for d in range(1, n_half):
        got.append(shift(lists[d], d, n_half))
    for r in range(1, n_aux // 2):
        near[r] = lax.ppermute(near[r], "aux", [(a, a ^ (2 * r)) for a in range(n_aux)])
    other = join(near, 1)
    other = swap(other, n_aux)
    own = prep(near, other)

    def roomy(got, spill):
        return merge(plan, got, ohalf, n_half, per)

    def crowded(levels):
        def run(got, spill):
            for level in spill[:levels]:
                got = got + [level[0]] + [shift(level[d], d, n_half) for d in range(1, n_half)]
            return merge(plan, got, ohalf, n_half, per)

        return run

    mine = lax.switch(crowd[0], [roomy] + [crowded(e + 1) for e in range(len(spill))], got, spill)
    ins, late = [], []
    for g in range(GROUPS):
        far = across(mine[g], 2, n_half)
        beside = across(mine[g], 1, n_half)
        parts = [mine[g], beside, far, across(far, 1, n_half)]
        z0 = pack(parts)
        r1 = plane(z0, n_aux, 0)
        r2 = plane(z0, n_aux, 1)
        late.append(plane(r1, n_aux, 1))
        early = join([z0, r1, r2])
        other = swap(early, n_aux)
        ins += amplitudes(own, early, other)
    late = join(late)
    late_other = swap(late, n_aux)
    density, energy = pair_terms(own, ins, late, late_other, occ_energy, plan, vir_energy, ohalf)
    return density[None, None], energy


def solution(mesh):
    fast = dict(mesh.shape) == {"aux": 8, "half": 4}
    in_specs = (P("aux", "half", None, None), P(), P(), P(), P())
    out_specs = (P("half", "aux", None, None), P("half", "aux"))
    return jax.shard_map(
        on_device if fast else any_mesh, mesh=mesh, in_specs=in_specs, out_specs=out_specs, check_vma=False
    )
```
